512 devices in a mesh: rows: 16 (over z), cols: 32 (over x, y, core).
Axes of the slice: x: 4, y: 4, z: 16, core: 2. Of those that a mesh axis runs over, the one named last changes fastest.
Arguments:
- boundary_in: bfloat16 [16, 32, 16, 256, 256], P('rows', 'cols'), may hold values from -6 to 6
- row_operator: bfloat16 [16, 32, 16, 16], P('rows', 'cols'), may hold values from -1.5 to 1.5
- charges: int32 [16, 32], P('rows', 'cols'), may hold values from 64 to 192
Outputs:
- boundary_out: bfloat16 [16, 32, 16, 256, 256], P('rows', 'cols')
- operator_grad: float32 [16, 32, 16, 16], P('rows', 'cols')
The draws below stay inside these ranges and needn't reach their ends.
All inputs are finite; a program needn't handle non-finite values.
Results may differ from the reference program's by a relative error of at most 0.005.
Values may be sent and summed in bfloat16 or wider, within the bound.
A program may use at most 64 MiB of HBM per device.

```python
import math
import jax
import jax.numpy as jnp
from jax import lax

CHI = 256
DD = 16
SITES = 32
SECTIONS = 16


def place_ends(values, rng, low, top_value):
    longest = values.shape.index(max(values.shape))
    spots = []
    for shift in (0, 1):
        where = [jax.random.randint(jax.random.fold_in(rng, axis), (), 0, length) for axis, length in enumerate(values.shape)]
        where[longest] = (where[longest] + shift) % values.shape[longest]
        spots.append(tuple(where))
    return values.at[spots[0]].set(low).at[spots[1]].set(top_value)


def level_of(key, shape, split, least, high):
    loudness, own = 1.0, jax.random.fold_in(key, 6)
    for position, parts in split:
        steps = jnp.exp(jax.random.uniform(jax.random.fold_in(own, position), (parts,), jnp.float32, least / len(split), high / len(split)))
        loudness = loudness * jnp.repeat(steps, shape[position] // parts).reshape([-1 if axis == position else 1 for axis in range(len(shape))])
    return loudness


def noise(stream_key, shape, deviation, bound, cuts=(), kind=jnp.bfloat16):
    array = jax.random.normal(stream_key, shape, jnp.float32) * deviation
    if len(cuts) > 0:
        array = level_of(stream_key, shape, cuts, -0.22, 0.18) * array
    return jnp.clip(array, min=-bound, max=bound).astype(kind)


def setup_inputs(seed: int = 0) -> dict:
    key_of = jax.random.split(jax.random.key(seed), 4)
    return {
        "boundary_in": noise(key_of[0], (SECTIONS, SITES, DD, CHI, CHI), 1.0, 6.0, ((0, 16), (1, 32))),
        "row_operator": noise(key_of[1], (SECTIONS, SITES, DD, DD), DD ** -0.5, 1.5, ((0, 16), (1, 32))),
        "charges": place_ends(jax.random.randint(key_of[2], (SECTIONS, SITES), CHI // 4, 3 * CHI // 4 + 1), jax.random.fold_in(key_of[2], 1), CHI // 4, (3 * CHI // 4 + 1) - 1).astype(jnp.int32),
    }


def keep_mask(charge_row, phys_dim, bond_dim):
    phys_odd = jnp.arange(phys_dim) >= phys_dim // 2
    left_odd = jnp.arange(bond_dim)[None, :] >= charge_row[:, None]
    right_odd = jnp.arange(bond_dim) >= bond_dim // 2
    parity = jnp.logical_xor(jnp.logical_xor(phys_odd[None, :, None, None], left_odd[:, None, :, None]), right_odd[None, None, None, :])
    return jnp.logical_not(parity)

def compress_section(packed):
    bound_sec, oper_sec, charge_sec = packed
    applied = jnp.einsum('spq,sqlc->splc', oper_sec.astype(jnp.float32), bound_sec.astype(jnp.float32))
    applied = jnp.where(keep_mask(charge_sec, DD, CHI), applied, 0.0).astype(jnp.bfloat16)
    flat_rows = applied.reshape(-1, CHI)
    gram = jnp.dot(flat_rows.T.astype(jnp.float32), flat_rows.astype(jnp.float32), preferred_element_type=jnp.float32) / (SITES * DD * CHI / 2.0)
    factor = jnp.linalg.cholesky(gram)
    inverse = jax.scipy.linalg.solve_triangular(factor, jnp.eye(CHI, dtype=jnp.float32), lower=True)
    result = jnp.dot(flat_rows.astype(jnp.float32), inverse.T, precision=lax.Precision.HIGHEST)
    return result.astype(jnp.bfloat16).reshape(SITES, DD, CHI, CHI)

def adjoint_section(packed):
    bound_sec, own_out, next_out = packed
    own_flat = own_out.reshape(-1, CHI)
    next_flat = next_out.reshape(-1, CHI)
    mix_scale = 2.0 / (CHI * math.sqrt(SITES * DD))
    correlation = (jnp.dot(own_flat.T.astype(jnp.float32), next_flat.astype(jnp.float32), preferred_element_type=jnp.float32) * mix_scale).astype(jnp.bfloat16)
    adjoint = jnp.dot(next_flat.astype(jnp.float32), correlation.T.astype(jnp.float32), preferred_element_type=jnp.float32).astype(jnp.bfloat16)
    adjoint = adjoint.reshape(SITES, DD, CHI, CHI)
    gradient = jnp.einsum('splc,sqlc->spq', adjoint.astype(jnp.float32), bound_sec.astype(jnp.float32))
    return gradient / CHI

def reference(boundary_in, row_operator, charges):
    boundary_out = lax.map(compress_section, (boundary_in, row_operator, charges))
    shifted = jnp.concatenate([boundary_out[1:], jnp.zeros_like(boundary_out[:1])], axis=0)
    operator_grad = lax.map(adjoint_section, (boundary_in, boundary_out, shifted))
    return (boundary_out, operator_grad)
```

```python
import functools
import math

import jax
import jax.numpy as jnp
from jax import lax
from jax.experimental import pallas as pl
from jax.experimental.pallas import tpu as pltpu
from jax.sharding import PartitionSpec as P

HIGH = lax.Precision.HIGHEST
MESH = pl.DeviceIdType.MESH


def from_next(value):
    count = lax.axis_size("rows")
    return lax.ppermute(value, "rows", [(r + 1, r) for r in range(count - 1)])


def sum_kernel(count, part_ref, out_ref, landed, whole, send_a, recv_a, send_b, recv_b):
    me = lax.axis_index("cols")

    def after(k):
        return lax.rem(me + k, count)

    def before(k):
        return lax.rem(me + count - k, count)

    barrier = pltpu.get_barrier_semaphore()

    @pl.loop(1, count)
    def _(k):
        pl.semaphore_signal(barrier, inc=1, device_id={"cols": after(k)}, device_id_type=MESH)

    pl.semaphore_wait(barrier, count - 1)

    def scatter(k):
        return pltpu.make_async_remote_copy(
            src_ref=part_ref.at[after(k)],
            dst_ref=landed.at[k],
            send_sem=send_a.at[k],
            recv_sem=recv_a.at[k],
            device_id={"cols": after(k)},
            device_id_type=MESH,
        )

    @pl.loop(1, count)
    def _(k):
        scatter(k).start()

    landed[0] = part_ref[me]

    @pl.loop(1, count)
    def _(k):
        scatter(k).wait_recv()

    whole[me] = jnp.sum(landed[...], axis=0)

    def gather(k, owner):
        return pltpu.make_async_remote_copy(
            src_ref=whole.at[owner],
            dst_ref=whole.at[owner],
            send_sem=send_b.at[k],
            recv_sem=recv_b.at[k],
            device_id={"cols": after(k)},
            device_id_type=MESH,
        )

    @pl.loop(1, count)
    def _(k):
        gather(k, me).start()

    @pl.loop(1, count)
    def _(k):
        gather(k, before(k)).wait_recv()

    out_ref[...] = whole[...]

    @pl.loop(1, count)
    def _(k):
        scatter(k).wait_send()
        gather(k, me).wait_send()


def sum_over_cols(part, collective_id):
    count = lax.axis_size("cols")
    shape = part.shape
    pieces = (count, part.size // count // 128, 128)
    total = pl.pallas_call(
        functools.partial(sum_kernel, count),
        out_shape=jax.ShapeDtypeStruct(pieces, jnp.float32),
        in_specs=[pl.BlockSpec(memory_space=pltpu.VMEM)],
        out_specs=pl.BlockSpec(memory_space=pltpu.VMEM),
        scratch_shapes=[
            pltpu.VMEM(pieces, jnp.float32),
            pltpu.VMEM(pieces, jnp.float32),
            pltpu.SemaphoreType.DMA((count,)),
            pltpu.SemaphoreType.DMA((count,)),
            pltpu.SemaphoreType.DMA((count,)),
            pltpu.SemaphoreType.DMA((count,)),
        ],
        compiler_params=pltpu.CompilerParams(collective_id=collective_id, has_side_effects=True),
        cost_estimate=pl.CostEstimate(flops=part.size, bytes_accessed=16 * part.size, transcendentals=0),
        name="sum_over_cols",
    )(part.reshape(pieces))
    return total.reshape(shape)


def odd_rows(charge, phys_dim, bond_dim):
    phys_odd = jnp.arange(phys_dim) >= phys_dim // 2
    left_odd = jnp.arange(bond_dim) >= charge
    return jnp.logical_xor(phys_odd[:, None], left_odd[None, :]).reshape(-1, 1)


def unpack(packed, odd):
    zero = jnp.zeros_like(packed)
    return jnp.concatenate([jnp.where(odd, zero, packed), jnp.where(odd, packed, zero)], axis=1)


def shards(boundary_in, row_operator, charges):
    stored, oper, charge = boundary_in[0, 0], row_operator[0, 0], charges[0, 0]
    phys_dim, bond_dim = stored.shape[0], stored.shape[2]
    half, phalf = bond_dim // 2, phys_dim // 2
    all_sites = lax.axis_size("cols")
    left_odd = (jnp.arange(bond_dim) >= charge)[None, :, None]
    low, high = stored[:, :, :half], stored[:, :, half:]
    applied = jnp.concatenate(
        [
            jnp.einsum("pq,qlc->plc", oper[:phalf], jnp.where(left_odd, high, low), preferred_element_type=jnp.float32),
            jnp.einsum("pq,qlc->plc", oper[phalf:], jnp.where(left_odd, low, high), preferred_element_type=jnp.float32),
        ]
    )
    packed = applied.astype(jnp.bfloat16).reshape(-1, half)
    packed_next = from_next(packed)
    charge_next = from_next(charges)[0, 0]
    odd = odd_rows(charge, phys_dim, bond_dim)
    flat = unpack(packed, odd)
    gram = lax.dot_general(packed, flat, (((0,), (0,)), ((), ())), preferred_element_type=jnp.float32)
    gram = sum_over_cols(gram, 0) / (all_sites * phys_dim * bond_dim / 2.0)
    grams = jnp.stack([gram[:, :half], gram[:, half:]])
    factor = jnp.linalg.cholesky(grams)
    eye = jnp.broadcast_to(jnp.eye(half, dtype=jnp.float32), factor.shape)
    inverse = lax.linalg.triangular_solve(factor, eye, left_side=True, lower=True)
    inverse_next = from_next(inverse)

    def compress(rows, inv, rows_odd):
        both = jnp.concatenate([inv[0].T, inv[1].T], axis=1)
        out = jnp.dot(rows, both, precision=HIGH, preferred_element_type=jnp.float32)
        right_odd = (jnp.arange(bond_dim) >= half)[None, :]
        return jnp.where(rows_odd == right_odd, out, 0.0).astype(jnp.bfloat16)

    compressed = compress(packed, inverse, odd)
    odd_next = odd_rows(charge_next, phys_dim, bond_dim)
    flat_next = unpack(packed_next, odd_next)
    cross = lax.dot_general(flat, flat_next, (((0,), (0,)), ((), ())), preferred_element_type=jnp.float32)
    cross = sum_over_cols(cross, 1)

    def block(inv):
        zero = jnp.zeros_like(inv[0])
        return jnp.concatenate([jnp.concatenate([inv[0], zero], 1), jnp.concatenate([zero, inv[1]], 1)], 0)

    mix_scale = 2.0 / (bond_dim * math.sqrt(all_sites * phys_dim))
    correlation = jnp.dot(block(inverse), cross, precision=HIGH)
    correlation = jnp.dot(correlation, block(inverse_next).T, precision=HIGH)
    correlation = (correlation * mix_scale).astype(jnp.bfloat16)
    compressed_next = compress(packed_next, inverse_next, odd_next)
    adjoint = jnp.dot(compressed_next, correlation.T, preferred_element_type=jnp.float32).astype(jnp.bfloat16)
    adjoint = adjoint.reshape(phys_dim, bond_dim, bond_dim)
    gradient = jnp.einsum("plc,qlc->pq", adjoint, stored, preferred_element_type=jnp.float32) / bond_dim
    return (compressed.reshape(boundary_in.shape), gradient[None, None])


def solution(mesh):
    return jax.shard_map(
        shards,
        mesh=mesh,
        in_specs=(
            P("rows", "cols", None, None, None),
            P("rows", "cols", None, None),
            P("rows", "cols"),
        ),
        out_specs=(P("rows", "cols", None, None, None), P("rows", "cols", None, None)),
        check_vma=False,
    )
```

```python
import functools
import math

import jax
import jax.numpy as jnp
from jax import lax
from jax.experimental import pallas as pl
from jax.experimental.pallas import tpu as pltpu
from jax.sharding import PartitionSpec as P

HIGH = lax.Precision.HIGHEST
MESH = pl.DeviceIdType.MESH


def from_next(value):
    count = lax.axis_size("rows")
    return lax.ppermute(value, "rows", [(r + 1, r) for r in range(count - 1)])


def sum_kernel(count, part_ref, out_ref, landed, whole, send_a, recv_a, send_b, recv_b):
    me = lax.axis_index("cols")

    def after(k):
        return lax.rem(me + k, count)

    def before(k):
        return lax.rem(me + count - k, count)

    barrier = pltpu.get_barrier_semaphore()

    @pl.loop(1, count)
    def _(k):
        pl.semaphore_signal(barrier, inc=1, device_id={"cols": after(k)}, device_id_type=MESH)

    pl.semaphore_wait(barrier, count - 1)

    def scatter(k):
        return pltpu.make_async_remote_copy(
            src_ref=part_ref.at[after(k)],
            dst_ref=landed.at[k],
            send_sem=send_a.at[k],
            recv_sem=recv_a.at[k],
            device_id={"cols": after(k)},
            device_id_type=MESH,
        )

    @pl.loop(1, count)
    def _(k):
        scatter(k).start()

    landed[0] = part_ref[me]

    @pl.loop(1, count)
    def _(k):
        scatter(k).wait_recv()

    whole[me] = jnp.sum(landed[...], axis=0)

    def gather(k, owner):
        return pltpu.make_async_remote_copy(
            src_ref=whole.at[owner],
            dst_ref=whole.at[owner],
            send_sem=send_b.at[k],
            recv_sem=recv_b.at[k],
            device_id={"cols": after(k)},
            device_id_type=MESH,
        )

    @pl.loop(1, count)
    def _(k):
        gather(k, me).start()

    @pl.loop(1, count)
    def _(k):
        gather(k, before(k)).wait_recv()

    out_ref[...] = whole[...]

    @pl.loop(1, count)
    def _(k):
        scatter(k).wait_send()
        gather(k, me).wait_send()


def sum_over_cols(part, collective_id):
    count = lax.axis_size("cols")
    shape = part.shape
    pieces = (count, part.size // count // 128, 128)
    total = pl.pallas_call(
        functools.partial(sum_kernel, count),
        out_shape=jax.ShapeDtypeStruct(pieces, jnp.float32),
        in_specs=[pl.BlockSpec(memory_space=pltpu.VMEM)],
        out_specs=pl.BlockSpec(memory_space=pltpu.VMEM),
        scratch_shapes=[
            pltpu.VMEM(pieces, jnp.float32),
            pltpu.VMEM(pieces, jnp.float32),
            pltpu.SemaphoreType.DMA((count,)),
            pltpu.SemaphoreType.DMA((count,)),
            pltpu.SemaphoreType.DMA((count,)),
            pltpu.SemaphoreType.DMA((count,)),
        ],
        compiler_params=pltpu.CompilerParams(collective_id=collective_id, has_side_effects=True),
        cost_estimate=pl.CostEstimate(flops=part.size, bytes_accessed=16 * part.size, transcendentals=0),
        name="sum_over_cols",
    )(part.reshape(pieces))
    return total.reshape(shape)


def split3(x):
    high = x.astype(jnp.bfloat16).astype(jnp.float32)
    rest = x - high
    mid = rest.astype(jnp.bfloat16).astype(jnp.float32)
    return high, mid, rest - mid


def invert_factor(state, size):
    step = 8
    blocks = range(state.shape[0])
    lane = lax.broadcasted_iota(jnp.int32, (step, size), 1)
    sub = lax.broadcasted_iota(jnp.int32, (step, size), 0)
    lane_all = lax.broadcasted_iota(jnp.int32, (size, size), 1)
    for base in range(0, size, step):
        stop = base + step
        own = (lane >= base) & (lane < stop)
        for b in blocks:
            rows = state[b, base:stop, :]
            columns = [jnp.broadcast_to(rows[:, base + k : base + k + 1], (step, size)) for k in range(step)]
            unit = jnp.where(lane == sub + base, 1.0, 0.0)
            pivots = jnp.ones((step, size), jnp.float32)
            for k in range(step):
                pivot = jnp.broadcast_to(columns[k][k : k + 1, :], (step, size))
                pivots = jnp.where(sub == k, pivot, pivots)
                factor = jnp.where(sub > k, columns[k] / pivot, 0.0)
                for later in range(k + 1, step):
                    columns[later] = columns[later] - factor * jnp.broadcast_to(columns[later][k : k + 1, :], (step, size))
                rows = rows - factor * jnp.broadcast_to(rows[k : k + 1, :], (step, size))
                unit = unit - factor * jnp.broadcast_to(unit[k : k + 1, :], (step, size))
            done = jnp.where(own, unit, rows)
            if stop < size:
                lh, lm, ll = split3(rows / pivots)
                rh, rm, rl = split3(done)
                left = jnp.concatenate([lh, lh, lm, lh, ll, lm], axis=0).astype(jnp.bfloat16)
                right = jnp.concatenate([rh, rm, rh, rl, rh, rm], axis=0).astype(jnp.bfloat16)
                update = lax.dot_general(left, right, (((0,), (0,)), ((), ())), preferred_element_type=jnp.float32)
                below = state[b, stop:, :]
                inside = (lane_all[stop:] >= base) & (lane_all[stop:] < stop)
                state[b, stop:, :] = jnp.where(inside, 0.0, below) - update[stop:]
            state[b, base:stop, :] = jnp.where(lane <= sub + base, done * lax.rsqrt(pivots), 0.0)


def middle_kernel(count, sections, scale, gram_ref, part_ref, inverse_ref, next_ref, total_ref, state, arrived, landed, whole, send_a, recv_a, send_b, recv_b, send_c, recv_c):
    me = lax.axis_index("cols")
    row = lax.axis_index("rows")
    size = state.shape[1]
    below = lax.rem(row + sections - 1, sections)
    above = lax.rem(row + 1, sections)

    def after(k):
        return lax.rem(me + k, count)

    def before(k):
        return lax.rem(me + count - k, count)

    barrier = pltpu.get_barrier_semaphore()
    pl.semaphore_signal(barrier, inc=1, device_id={"rows": below}, device_id_type=MESH)
    pl.semaphore_signal(barrier, inc=1, device_id={"rows": above}, device_id_type=MESH)

    @pl.loop(1, count)
    def _(k):
        pl.semaphore_signal(barrier, inc=1, device_id={"cols": after(k)}, device_id_type=MESH)

    pl.semaphore_wait(barrier, count + 1)

    def scatter(k):
        return pltpu.make_async_remote_copy(
            src_ref=part_ref.at[after(k)],
            dst_ref=landed.at[k],
            send_sem=send_a.at[k],
            recv_sem=recv_a.at[k],
            device_id={"cols": after(k)},
            device_id_type=MESH,
        )

    @pl.loop(1, count)
    def _(k):
        scatter(k).start()

    landed[0] = part_ref[me]
    state[0] = gram_ref[:, :size] * scale
    state[1] = gram_ref[:, size:] * scale
    invert_factor(state, size)
    down = pltpu.make_async_remote_copy(
        src_ref=state,
        dst_ref=arrived,
        send_sem=send_c,
        recv_sem=recv_c,
        device_id={"rows": below},
        device_id_type=MESH,
    )
    down.start()

    @pl.loop(1, count)
    def _(k):
        scatter(k).wait_recv()

    whole[me] = jnp.sum(landed[...], axis=0)

    def gather(k, owner):
        return pltpu.make_async_remote_copy(
            src_ref=whole.at[owner],
            dst_ref=whole.at[owner],
            send_sem=send_b.at[k],
            recv_sem=recv_b.at[k],
            device_id={"cols": after(k)},
            device_id_type=MESH,
        )

    @pl.loop(1, count)
    def _(k):
        gather(k, me).start()

    inverse_ref[...] = state[...]

    @pl.loop(1, count)
    def _(k):
        gather(k, before(k)).wait_recv()

    total_ref[...] = whole[...]
    down.wait_recv()
    next_ref[...] = arrived[...]
    down.wait_send()

    @pl.loop(1, count)
    def _(k):
        scatter(k).wait_send()
        gather(k, me).wait_send()


def invert_and_sum(gram, scale, part, collective_id):
    count, sections = lax.axis_size("cols"), lax.axis_size("rows")
    size = gram.shape[0]
    blocks = jax.ShapeDtypeStruct((2, size, size), jnp.float32)
    pieces = jax.ShapeDtypeStruct((count, part.size // count // 128, 128), jnp.float32)
    vmem = pl.BlockSpec(memory_space=pltpu.VMEM)
    inverse, following, total = pl.pallas_call(
        functools.partial(middle_kernel, count, sections, scale),
        out_shape=(blocks, blocks, pieces),
        in_specs=[vmem, vmem],
        out_specs=(vmem, vmem, vmem),
        scratch_shapes=[
            pltpu.VMEM(blocks.shape, jnp.float32),
            pltpu.VMEM(blocks.shape, jnp.float32),
            pltpu.VMEM(pieces.shape, jnp.float32),
            pltpu.VMEM(pieces.shape, jnp.float32),
            pltpu.SemaphoreType.DMA((count,)),
            pltpu.SemaphoreType.DMA((count,)),
            pltpu.SemaphoreType.DMA((count,)),
            pltpu.SemaphoreType.DMA((count,)),
            pltpu.SemaphoreType.DMA,
            pltpu.SemaphoreType.DMA,
        ],
        compiler_params=pltpu.CompilerParams(collective_id=collective_id, has_side_effects=True),
        cost_estimate=pl.CostEstimate(flops=part.size, bytes_accessed=16 * part.size, transcendentals=0),
        name="invert_and_sum",
    )(gram, part.reshape(pieces.shape))
    is_last = lax.axis_index("rows") == sections - 1
    return inverse, jnp.where(is_last, 0.0, following), total.reshape(part.shape)


def odd_rows(charge, phys_dim, bond_dim):
    phys_odd = jnp.arange(phys_dim) >= phys_dim // 2
    left_odd = jnp.arange(bond_dim) >= charge
    return jnp.logical_xor(phys_odd[:, None], left_odd[None, :]).reshape(-1, 1)


def unpack(packed, odd):
    zero = jnp.zeros_like(packed)
    return jnp.concatenate([jnp.where(odd, zero, packed), jnp.where(odd, packed, zero)], axis=1)


def shards(boundary_in, row_operator, charges):
    stored, oper, charge = boundary_in[0, 0], row_operator[0, 0], charges[0, 0]
    phys_dim, bond_dim = stored.shape[0], stored.shape[2]
    half, phalf = bond_dim // 2, phys_dim // 2
    all_sites = lax.axis_size("cols")
    left_odd = (jnp.arange(bond_dim) >= charge)[None, :, None]
    low, high = stored[:, :, :half], stored[:, :, half:]
    applied = jnp.concatenate(
        [
            jnp.einsum("pq,qlc->plc", oper[:phalf], jnp.where(left_odd, high, low), preferred_element_type=jnp.float32),
            jnp.einsum("pq,qlc->plc", oper[phalf:], jnp.where(left_odd, low, high), preferred_element_type=jnp.float32),
        ]
    )
    packed = applied.astype(jnp.bfloat16).reshape(-1, half)
    packed_next = from_next(packed)
    charge_next = from_next(charges)[0, 0]
    odd = odd_rows(charge, phys_dim, bond_dim)
    flat = unpack(packed, odd)
    gram = lax.dot_general(packed, flat, (((0,), (0,)), ((), ())), preferred_element_type=jnp.float32)
    gram = sum_over_cols(gram, 0)
    odd_next = odd_rows(charge_next, phys_dim, bond_dim)
    flat_next = unpack(packed_next, odd_next)
    cross = lax.dot_general(flat, flat_next, (((0,), (0,)), ((), ())), preferred_element_type=jnp.float32)
    scale = 2.0 / (all_sites * phys_dim * bond_dim)
    inverse, inverse_next, cross = invert_and_sum(gram, scale, cross, 1)

    def compress(rows, inv, rows_odd):
        both = jnp.concatenate([inv[0].T, inv[1].T], axis=1)
        out = jnp.dot(rows, both, precision=HIGH, preferred_element_type=jnp.float32)
        right_odd = (jnp.arange(bond_dim) >= half)[None, :]
        return jnp.where(rows_odd == right_odd, out, 0.0).astype(jnp.bfloat16)

    compressed = compress(packed, inverse, odd)

    def block(inv):
        zero = jnp.zeros_like(inv[0])
        return jnp.concatenate([jnp.concatenate([inv[0], zero], 1), jnp.concatenate([zero, inv[1]], 1)], 0)

    mix_scale = 2.0 / (bond_dim * math.sqrt(all_sites * phys_dim))
    correlation = jnp.dot(block(inverse), cross, precision=HIGH)
    correlation = jnp.dot(correlation, block(inverse_next).T, precision=HIGH)
    correlation = (correlation * mix_scale).astype(jnp.bfloat16)
    compressed_next = compress(packed_next, inverse_next, odd_next)
    adjoint = jnp.dot(compressed_next, correlation.T, preferred_element_type=jnp.float32).astype(jnp.bfloat16)
    adjoint = adjoint.reshape(phys_dim, bond_dim, bond_dim)
    gradient = jnp.einsum("plc,qlc->pq", adjoint, stored, preferred_element_type=jnp.float32) / bond_dim
    return (compressed.reshape(boundary_in.shape), gradient[None, None])


def solution(mesh):
    return jax.shard_map(
        shards,
        mesh=mesh,
        in_specs=(
            P("rows", "cols", None, None, None),
            P("rows", "cols", None, None),
            P("rows", "cols"),
        ),
        out_specs=(P("rows", "cols", None, None, None), P("rows", "cols", None, None)),
        check_vma=False,
    )
```

```python
import functools
import math

import jax
import jax.numpy as jnp
from jax import lax
from jax.experimental import pallas as pl
from jax.experimental.pallas import tpu as pltpu
from jax.sharding import PartitionSpec as P

HIGH = lax.Precision.HIGHEST
MESH = pl.DeviceIdType.MESH


def split3(x):
    high = x.astype(jnp.bfloat16).astype(jnp.float32)
    rest = x - high
    mid = rest.astype(jnp.bfloat16).astype(jnp.float32)
    return high, mid, rest - mid


def invert_factor(state, size, first, last):
    step = 8
    blocks = range(state.shape[0])
    lane = lax.broadcasted_iota(jnp.int32, (step, size), 1)
    sub = lax.broadcasted_iota(jnp.int32, (step, size), 0)
    lane_all = lax.broadcasted_iota(jnp.int32, (size, size), 1)
    for base in range(first, last, step):
        stop = base + step
        own = (lane >= base) & (lane < stop)
        for b in blocks:
            rows = state[b, base:stop, :]
            columns = [jnp.broadcast_to(rows[:, base + k : base + k + 1], (step, size)) for k in range(step)]
            unit = jnp.where(lane == sub + base, 1.0, 0.0)
            pivots = jnp.ones((step, size), jnp.float32)
            for k in range(step):
                pivot = jnp.broadcast_to(columns[k][k : k + 1, :], (step, size))
                pivots = jnp.where(sub == k, pivot, pivots)
                factor = jnp.where(sub > k, columns[k] / pivot, 0.0)
                for later in range(k + 1, step):
                    columns[later] = columns[later] - factor * jnp.broadcast_to(columns[later][k : k + 1, :], (step, size))
                rows = rows - factor * jnp.broadcast_to(rows[k : k + 1, :], (step, size))
                unit = unit - factor * jnp.broadcast_to(unit[k : k + 1, :], (step, size))
            done = jnp.where(own, unit, rows)
            if stop < size:
                lh, lm, ll = split3(rows / pivots)
                rh, rm, rl = split3(done)
                left = jnp.concatenate([lh, lh, lm, lh, ll, lm], axis=0).astype(jnp.bfloat16)
                right = jnp.concatenate([rh, rm, rh, rl, rh, rm], axis=0).astype(jnp.bfloat16)
                update = lax.dot_general(left, right, (((0,), (0,)), ((), ())), preferred_element_type=jnp.float32)
                below = state[b, stop:, :]
                inside = (lane_all[stop:] >= base) & (lane_all[stop:] < stop)
                state[b, stop:, :] = jnp.where(inside, 0.0, below) - update[stop:]
            state[b, base:stop, :] = jnp.where(lane <= sub + base, done * lax.rsqrt(pivots), 0.0)


def exact_dot(rows, weights):
    high, mid, low = split3(weights)
    pair = jnp.concatenate([high, mid], axis=0).astype(jnp.bfloat16)
    twice = jnp.concatenate([rows, rows], axis=1)
    out = jnp.dot(twice, pair, preferred_element_type=jnp.float32)
    return out + jnp.dot(rows, low.astype(jnp.bfloat16), preferred_element_type=jnp.float32)


def unpack(rows, odd):
    wide = rows.astype(jnp.float32)
    return jnp.concatenate([jnp.where(odd, 0.0, wide), jnp.where(odd, wide, 0.0)], axis=1).astype(jnp.bfloat16)


def mask_halves(out, odd):
    half = out.shape[1] // 2
    return jnp.concatenate([jnp.where(odd, 0.0, out[:, :half]), jnp.where(odd, out[:, half:], 0.0)], axis=1).astype(jnp.bfloat16)


def whole_kernel(
    count, sections, phys, bond, scale, mix_scale,
    packed_ref, stored_hbm, charge_ref,
    out_ref, grad_ref,
    stored, ordered, packed_next, compressed_next, charge_own, charge_next,
    state, inverse_next, gram_part, gram_land, gram_all, cross_part, cross_land, cross_all,
    send_a, recv_a, send_b, recv_b, send_c, recv_c, send_d, recv_d, send_r, recv_r, load_sem,
):
    me = lax.axis_index("cols")
    row = lax.axis_index("rows")
    half = bond // 2
    below = lax.rem(row + sections - 1, sections)
    above = lax.rem(row + 1, sections)

    def after(k):
        return lax.rem(me + k, count)

    def before(k):
        return lax.rem(me + count - k, count)

    barrier = pltpu.get_barrier_semaphore()
    pl.semaphore_signal(barrier, inc=1, device_id={"rows": below}, device_id_type=MESH)
    pl.semaphore_signal(barrier, inc=1, device_id={"rows": above}, device_id_type=MESH)

    @pl.loop(1, count)
    def _(k):
        pl.semaphore_signal(barrier, inc=1, device_id={"cols": after(k)}, device_id_type=MESH)

    load = pltpu.make_async_copy(stored_hbm, stored, load_sem)
    load.start()
    charge = charge_ref[0, 0]
    charge_own[...] = jnp.full(charge_own.shape, charge, jnp.int32)
    tile = 2 * bond
    tiles = phys // 2
    place = lax.broadcasted_iota(jnp.int32, (tile, half), 0)

    def odd_rows(step, charge):
        left_odd = lax.rem(place, bond) >= charge
        phys_odd = (2 * step + place // bond) >= phys // 2
        return left_odd != phys_odd

    def rows_of(step):
        return pl.ds(pl.multiple_of(step * tile, tile), tile)

    def gram_step(step, total):
        rows = packed_ref[rows_of(step), :]
        flat = unpack(rows, odd_rows(step, charge))
        return total + lax.dot_general(rows, flat, (((0,), (0,)), ((), ())), preferred_element_type=jnp.float32)

    gram = lax.fori_loop(0, tiles, gram_step, jnp.zeros((half, bond), jnp.float32))
    gram_part[: count // 2] = gram[:, :half].reshape(count // 2, -1, half)
    gram_part[count // 2 :] = gram[:, half:].reshape(count // 2, -1, half)
    pl.semaphore_wait(barrier, count + 1)

    def to_below(source, target, index):
        return pltpu.make_async_remote_copy(
            src_ref=source, dst_ref=target, send_sem=send_r.at[index], recv_sem=recv_r.at[index],
            device_id={"rows": below}, device_id_type=MESH,
        )

    def scatter(k, part, land, send, recv):
        return pltpu.make_async_remote_copy(
            src_ref=part.at[after(k)], dst_ref=land.at[k], send_sem=send.at[k], recv_sem=recv.at[k],
            device_id={"cols": after(k)}, device_id_type=MESH,
        )

    def gather(k, owner, whole, send, recv):
        return pltpu.make_async_remote_copy(
            src_ref=whole.at[owner], dst_ref=whole.at[owner], send_sem=send.at[k], recv_sem=recv.at[k],
            device_id={"cols": after(k)}, device_id_type=MESH,
        )

    @pl.loop(1, count)
    def _(k):
        scatter(k, gram_part, gram_land, send_a, recv_a).start()

    rows_down = to_below(packed_ref, packed_next, 0)
    rows_down.start()
    charge_down = to_below(charge_own, charge_next, 1)
    charge_down.start()
    gram_land[0] = gram_part[me]
    load.wait()
    group = bond // phys
    block = group * phys

    def reorder(step, source, target):
        left = pl.ds(pl.multiple_of(step * group, group), group)
        rows = source[:, left, :].astype(jnp.float32)
        rows = jnp.swapaxes(rows, 0, 1).reshape(block, rows.shape[2])
        target[pl.ds(pl.multiple_of(step * block, block), block), :] = rows.astype(jnp.bfloat16)

    @pl.loop(0, bond // group // 2)
    def _(step):
        reorder(step, stored, ordered)

    @pl.loop(1, count)
    def _(k):
        scatter(k, gram_part, gram_land, send_a, recv_a).wait_recv()

    gram_all[me] = jnp.sum(gram_land[...], axis=0)

    @pl.loop(1, count)
    def _(k):
        gather(k, me, gram_all, send_b, recv_b).start()

    @pl.loop(bond // group // 2, bond // group)
    def _(step):
        reorder(step, stored, ordered)

    @pl.loop(1, count)
    def _(k):
        gather(k, before(k), gram_all, send_b, recv_b).wait_recv()

    state[0] = gram_all[: count // 2].reshape(half, half) * scale
    state[1] = gram_all[count // 2 :].reshape(half, half) * scale
    invert_factor(state, half, 0, half // 4)
    rows_down.wait_recv()
    charge_down.wait_recv()
    charge_above = charge_next[0:1, :]

    def cross_step(step, total):
        flat = unpack(packed_ref[rows_of(step), :], odd_rows(step, charge))
        other = unpack(packed_next[rows_of(step), :], odd_rows(step, charge_above))
        return total + lax.dot_general(flat, other, (((0,), (0,)), ((), ())), preferred_element_type=jnp.float32)

    cross = lax.fori_loop(0, tiles, cross_step, jnp.zeros((bond, bond), jnp.float32))
    cross_part[: count // 2] = cross[:, :half].reshape(count // 2, -1, half)
    cross_part[count // 2 :] = cross[:, half:].reshape(count // 2, -1, half)

    @pl.loop(1, count)
    def _(k):
        scatter(k, cross_part, cross_land, send_c, recv_c).start()

    cross_land[0] = cross_part[me]
    invert_factor(state, half, half // 4, half)
    inverse_down = to_below(state, inverse_next, 2)
    inverse_down.start()

    @pl.loop(1, count)
    def _(k):
        scatter(k, cross_part, cross_land, send_c, recv_c).wait_recv()

    cross_all[me] = jnp.sum(cross_land[...], axis=0)

    @pl.loop(1, count)
    def _(k):
        gather(k, me, cross_all, send_d, recv_d).start()

    own = jnp.concatenate([state[0].T, state[1].T], axis=1)

    @pl.loop(0, tiles)
    def _(step):
        out = exact_dot(packed_ref[rows_of(step), :], own)
        out_ref[rows_of(step), :] = mask_halves(out, odd_rows(step, charge))

    inverse_down.wait_recv()
    following = jnp.concatenate([inverse_next[0].T, inverse_next[1].T], axis=1)
    next_rows = packed_next.reshape(phys, bond, half)
    spot = lax.broadcasted_iota(jnp.int32, (block, half), 0)

    @pl.loop(0, bond // group)
    def _(step):
        left = pl.ds(pl.multiple_of(step * group, group), group)
        rows = jnp.swapaxes(next_rows[:, left, :].astype(jnp.float32), 0, 1).reshape(block, half)
        odd = ((step * group + spot // phys) >= charge_above) != (lax.rem(spot, phys) >= phys // 2)
        out = exact_dot(rows.astype(jnp.bfloat16), following)
        compressed_next[pl.ds(pl.multiple_of(step * block, block), block), :] = mask_halves(out, odd)

    @pl.loop(1, count)
    def _(k):
        gather(k, before(k), cross_all, send_d, recv_d).wait_recv()

    total = jnp.concatenate(
        [cross_all[: count // 2].reshape(bond, half), cross_all[count // 2 :].reshape(bond, half)], axis=1
    )
    upper = jnp.concatenate(
        [
            jnp.dot(state[0], total[:half], precision=HIGH, preferred_element_type=jnp.float32),
            jnp.dot(state[1], total[half:], precision=HIGH, preferred_element_type=jnp.float32),
        ],
        axis=0,
    )
    turn = (((1,), (1,)), ((), ()))
    correlation = jnp.concatenate(
        [
            lax.dot_general(upper[:, :half], inverse_next[0], turn, precision=HIGH, preferred_element_type=jnp.float32),
            lax.dot_general(upper[:, half:], inverse_next[1], turn, precision=HIGH, preferred_element_type=jnp.float32),
        ],
        axis=1,
    )
    mixing = (correlation * mix_scale).T.astype(jnp.bfloat16)

    def gradient_step(step, total):
        rows = pl.ds(pl.multiple_of(step * block, block), block)
        adjoint = jnp.dot(compressed_next[rows, :], mixing, preferred_element_type=jnp.float32).astype(jnp.bfloat16)
        return total + lax.dot_general(adjoint, ordered[rows, :], turn, preferred_element_type=jnp.float32)

    pairs = lax.fori_loop(0, bond // group, gradient_step, jnp.zeros((block, block), jnp.float32))
    down = lax.broadcasted_iota(jnp.int32, (block, block), 0)
    across = lax.broadcasted_iota(jnp.int32, (block, block), 1)
    pairs = jnp.where(down // phys == across // phys, pairs, 0.0).reshape(group, phys, block).sum(axis=0)
    tall = lax.broadcasted_iota(jnp.int32, (block, phys), 0)
    wide = lax.broadcasted_iota(jnp.int32, (block, phys), 1)
    fold = jnp.where(lax.rem(tall, phys) == wide, 1.0, 0.0)
    gradient = jnp.dot(pairs, fold, precision=HIGH, preferred_element_type=jnp.float32)
    grad_ref[...] = jnp.where(row == sections - 1, 0.0, gradient / bond)
    rows_down.wait_send()
    charge_down.wait_send()
    inverse_down.wait_send()

    @pl.loop(1, count)
    def _(k):
        scatter(k, gram_part, gram_land, send_a, recv_a).wait_send()
        gather(k, me, gram_all, send_b, recv_b).wait_send()
        scatter(k, cross_part, cross_land, send_c, recv_c).wait_send()
        gather(k, me, cross_all, send_d, recv_d).wait_send()


def shards(boundary_in, row_operator, charges):
    stored, oper, charge = boundary_in[0, 0], row_operator[0, 0], charges[0, 0]
    phys, bond = stored.shape[0], stored.shape[2]
    half, phalf = bond // 2, phys // 2
    count, sections = lax.axis_size("cols"), lax.axis_size("rows")
    left_odd = (jnp.arange(bond) >= charge)[None, :, None]
    low, high = stored[:, :, :half], stored[:, :, half:]
    applied = jnp.concatenate(
        [
            jnp.einsum("pq,qlc->plc", oper[:phalf], jnp.where(left_odd, high, low), preferred_element_type=jnp.float32),
            jnp.einsum("pq,qlc->plc", oper[phalf:], jnp.where(left_odd, low, high), preferred_element_type=jnp.float32),
        ]
    )
    packed = applied.astype(jnp.bfloat16).reshape(-1, half)
    scale = 2.0 / (count * phys * bond)
    mix_scale = 2.0 / (bond * math.sqrt(count * phys))
    vmem = pl.BlockSpec(memory_space=pltpu.VMEM)
    gram_shape = (count, half * bond // count // half, half)
    cross_shape = (count, bond * bond // count // half, half)
    sems = pltpu.SemaphoreType.DMA((count,))
    compressed, gradient = pl.pallas_call(
        functools.partial(whole_kernel, count, sections, phys, bond, scale, mix_scale),
        out_shape=(
            jax.ShapeDtypeStruct((phys * bond, bond), jnp.bfloat16),
            jax.ShapeDtypeStruct((phys, phys), jnp.float32),
        ),
        in_specs=[vmem, pl.BlockSpec(memory_space=pl.ANY), pl.BlockSpec(memory_space=pltpu.SMEM)],
        out_specs=(vmem, vmem),
        scratch_shapes=[
            pltpu.VMEM((phys, bond, bond), jnp.bfloat16),
            pltpu.VMEM((phys * bond, bond), jnp.bfloat16),
            pltpu.VMEM((phys * bond, half), jnp.bfloat16),
            pltpu.VMEM((phys * bond, bond), jnp.bfloat16),
            pltpu.VMEM((8, half), jnp.int32),
            pltpu.VMEM((8, half), jnp.int32),
            pltpu.VMEM((2, half, half), jnp.float32),
            pltpu.VMEM((2, half, half), jnp.float32),
            pltpu.VMEM(gram_shape, jnp.float32),
            pltpu.VMEM(gram_shape, jnp.float32),
            pltpu.VMEM(gram_shape, jnp.float32),
            pltpu.VMEM(cross_shape, jnp.float32),
            pltpu.VMEM(cross_shape, jnp.float32),
            pltpu.VMEM(cross_shape, jnp.float32),
            sems, sems, sems, sems, sems, sems, sems, sems,
            pltpu.SemaphoreType.DMA((3,)),
            pltpu.SemaphoreType.DMA((3,)),
            pltpu.SemaphoreType.DMA,
        ],
        compiler_params=pltpu.CompilerParams(collective_id=0, has_side_effects=True),
        name="orthonormalise",
    )(packed, stored, charges)
    return (compressed.reshape(boundary_in.shape), gradient[None, None])


def solution(mesh):
    return jax.shard_map(
        shards,
        mesh=mesh,
        in_specs=(
            P("rows", "cols", None, None, None),
            P("rows", "cols", None, None),
            P("rows", "cols"),
        ),
        out_specs=(P("rows", "cols", None, None, None), P("rows", "cols", None, None)),
        check_vma=False,
    )
```

```python
import functools
import math

import jax
import jax.numpy as jnp
from jax import lax
from jax.experimental import pallas as pl
from jax.experimental.pallas import tpu as pltpu
from jax.sharding import PartitionSpec as P

HIGH = lax.Precision.HIGHEST
MESH = pl.DeviceIdType.MESH


def split3(x):
    high = x.astype(jnp.bfloat16).astype(jnp.float32)
    rest = x - high
    mid = rest.astype(jnp.bfloat16).astype(jnp.float32)
    return high, mid, rest - mid


def invert_factor(state, size, first, last):
    step = 8
    blocks = range(state.shape[0])
    lane = lax.broadcasted_iota(jnp.int32, (step, size), 1)
    sub = lax.broadcasted_iota(jnp.int32, (step, size), 0)
    lane_all = lax.broadcasted_iota(jnp.int32, (size, size), 1)
    for base in range(first, last, step):
        stop = base + step
        own = (lane >= base) & (lane < stop)
        for b in blocks:
            rows = state[b, base:stop, :]
            columns = [jnp.broadcast_to(rows[:, base + k : base + k + 1], (step, size)) for k in range(step)]
            unit = jnp.where(lane == sub + base, 1.0, 0.0)
            pivots = jnp.ones((step, size), jnp.float32)
            for k in range(step):
                pivot = jnp.broadcast_to(columns[k][k : k + 1, :], (step, size))
                pivots = jnp.where(sub == k, pivot, pivots)
                factor = jnp.where(sub > k, columns[k] / pivot, 0.0)
                for later in range(k + 1, step):
                    columns[later] = columns[later] - factor * jnp.broadcast_to(columns[later][k : k + 1, :], (step, size))
                rows = rows - factor * jnp.broadcast_to(rows[k : k + 1, :], (step, size))
                unit = unit - factor * jnp.broadcast_to(unit[k : k + 1, :], (step, size))
            done = jnp.where(own, unit, rows)
            if stop < size:
                lh, lm, ll = split3(rows / pivots)
                rh, rm, rl = split3(done)
                left = jnp.concatenate([lh, lh, lm, lh, ll, lm], axis=0).astype(jnp.bfloat16)
                right = jnp.concatenate([rh, rm, rh, rl, rh, rm], axis=0).astype(jnp.bfloat16)
                update = lax.dot_general(left, right, (((0,), (0,)), ((), ())), preferred_element_type=jnp.float32)
                below = state[b, stop:, :]
                inside = (lane_all[stop:] >= base) & (lane_all[stop:] < stop)
                state[b, stop:, :] = jnp.where(inside, 0.0, below) - update[stop:]
            state[b, base:stop, :] = jnp.where(lane <= sub + base, done * lax.rsqrt(pivots), 0.0)


def exact_parts(weights):
    high, mid, low = split3(weights)
    return jnp.concatenate([high, mid], axis=0).astype(jnp.bfloat16), low.astype(jnp.bfloat16)


def exact_dot(rows, parts):
    out = jnp.dot(jnp.concatenate([rows, rows], axis=1), parts[0], preferred_element_type=jnp.float32)
    return out + jnp.dot(rows, parts[1], preferred_element_type=jnp.float32)


def unpack(rows, odd):
    wide = rows.astype(jnp.float32)
    return jnp.concatenate([jnp.where(odd, 0.0, wide), jnp.where(odd, wide, 0.0)], axis=1).astype(jnp.bfloat16)


def mask_halves(out, odd):
    half = out.shape[1] // 2
    return jnp.concatenate([jnp.where(odd, 0.0, out[:, :half]), jnp.where(odd, out[:, half:], 0.0)], axis=1).astype(jnp.bfloat16)


def whole_kernel(
    count, sections, phys, bond, scale, mix_scale,
    even_ref, other_ref, stored_hbm, charge_ref,
    out_hbm, grad_ref,
    stored, ordered, packed_next, compressed_next, turned, adjoints, out, charge_own, charge_next,
    state, inverse_next, gram_part, gram_land, gram_all, cross_part, cross_land, cross_all,
    send_a, recv_a, send_b, recv_b, send_c, recv_c, send_d, recv_d, send_r, recv_r, load_sem, store_sem,
):
    me = lax.axis_index("cols")
    row = lax.axis_index("rows")
    half = bond // 2
    below = lax.rem(row + sections - 1, sections)
    above = lax.rem(row + 1, sections)

    def after(k):
        return lax.rem(me + k, count)

    def before(k):
        return lax.rem(me + count - k, count)

    barrier = pltpu.get_barrier_semaphore()
    pl.semaphore_signal(barrier, inc=1, device_id={"rows": below}, device_id_type=MESH)
    pl.semaphore_signal(barrier, inc=1, device_id={"rows": above}, device_id_type=MESH)

    @pl.loop(1, count)
    def _(k):
        pl.semaphore_signal(barrier, inc=1, device_id={"cols": after(k)}, device_id_type=MESH)

    load = pltpu.make_async_copy(stored_hbm, stored, load_sem)
    load.start()
    charge = charge_ref[0, 0]
    charge_own[...] = jnp.full(charge_own.shape, charge, jnp.int32)
    tile = 2 * bond
    tiles = phys // 2
    place = lax.broadcasted_iota(jnp.int32, (tile, half), 0)

    def odd_rows(step, charge):
        left_odd = lax.rem(place, bond) >= charge
        phys_odd = (2 * step + place // bond) >= phys // 2
        return left_odd != phys_odd

    packed = (even_ref, other_ref)
    per_half = tiles // 2

    def rows_of(step):
        return pl.ds(pl.multiple_of(step * tile, tile), tile)

    def to_below(source, target, index):
        return pltpu.make_async_remote_copy(
            src_ref=source, dst_ref=target, send_sem=send_r.at[index], recv_sem=recv_r.at[index],
            device_id={"rows": below}, device_id_type=MESH,
        )

    pieces = 4
    piece = phys * bond // pieces
    charge_down = to_below(charge_own, charge_next, pieces)
    rows_down = []
    for index in range(pieces):
        start = index * piece % (pieces // 2 * piece)
        source = packed[index * 2 // pieces].at[start : start + piece, :]
        rows_down.append(to_below(source, packed_next.at[index * piece : (index + 1) * piece, :], index))
    pl.semaphore_wait(barrier, count + 1)
    charge_down.start()
    for copy in rows_down:
        copy.start()
    lane_place = lax.broadcasted_iota(jnp.int32, (half, tile), 1)
    gram = jnp.zeros((half, bond), jnp.float32)
    for which in range(2):

        def gram_step(step, total, which=which):
            rows = packed[which][rows_of(step), :]
            across = rows.T
            flat = unpack(rows, odd_rows(which * per_half + step, charge))
            wide = across.astype(jnp.float32)
            odd = (lax.rem(lane_place, bond) >= charge) != (which == 1)
            columns = rows_of(which * per_half + step)
            turned[:half, columns] = jnp.where(odd, 0.0, wide).astype(jnp.bfloat16)
            turned[half:, columns] = jnp.where(odd, wide, 0.0).astype(jnp.bfloat16)
            return total + jnp.dot(across, flat, preferred_element_type=jnp.float32)

        gram = lax.fori_loop(0, per_half, gram_step, gram)
    gram_part[: count // 2] = gram[:, :half].reshape(count // 2, -1, half)
    gram_part[count // 2 :] = gram[:, half:].reshape(count // 2, -1, half)

    def scatter(k, part, land, send, recv):
        return pltpu.make_async_remote_copy(
            src_ref=part.at[after(k)], dst_ref=land.at[k], send_sem=send.at[k], recv_sem=recv.at[k],
            device_id={"cols": after(k)}, device_id_type=MESH,
        )

    def gather(k, owner, whole, send, recv):
        return pltpu.make_async_remote_copy(
            src_ref=whole.at[owner], dst_ref=whole.at[owner], send_sem=send.at[k], recv_sem=recv.at[k],
            device_id={"cols": after(k)}, device_id_type=MESH,
        )

    @pl.loop(1, count)
    def _(k):
        scatter(k, gram_part, gram_land, send_a, recv_a).start()

    gram_land[0] = gram_part[me]
    load.wait()
    group = bond // phys
    block = group * phys

    def reorder(step, source, target):
        left = pl.ds(pl.multiple_of(step * group, group), group)
        rows = source[:, left, :].astype(jnp.float32)
        rows = jnp.swapaxes(rows, 0, 1).reshape(block, rows.shape[2])
        target[pl.ds(pl.multiple_of(step * bond, bond), bond), :] = rows.T.astype(jnp.bfloat16)

    @pl.loop(0, bond // group // 2)
    def _(step):
        reorder(step, stored, ordered)

    @pl.loop(1, count)
    def _(k):
        scatter(k, gram_part, gram_land, send_a, recv_a).wait_recv()

    gram_all[me] = jnp.sum(gram_land[...], axis=0)

    @pl.loop(1, count)
    def _(k):
        gather(k, me, gram_all, send_b, recv_b).start()

    @pl.loop(bond // group // 2, bond // group)
    def _(step):
        reorder(step, stored, ordered)

    @pl.loop(1, count)
    def _(k):
        gather(k, before(k), gram_all, send_b, recv_b).wait_recv()

    state[0] = gram_all[: count // 2].reshape(half, half) * scale
    state[1] = gram_all[count // 2 :].reshape(half, half) * scale
    invert_factor(state, half, 0, half)
    inverse_down = to_below(state, inverse_next, pieces + 1)
    inverse_down.start()
    charge_down.wait_recv()
    charge_above = charge_next[0:1, :]
    cross = jnp.zeros((bond, bond), jnp.float32)
    for index in range(pieces):
        rows_down[index].wait_recv()
        first = index * piece // tile
        other = jnp.concatenate(
            [
                unpack(packed_next[step * tile : (step + 1) * tile, :], odd_rows(step, charge_above))
                for step in range(first, first + piece // tile)
            ],
            axis=0,
        )
        cross += jnp.dot(turned[:, index * piece : (index + 1) * piece], other, preferred_element_type=jnp.float32)
    cross_part[: count // 2] = cross[:, :half].reshape(count // 2, -1, half)
    cross_part[count // 2 :] = cross[:, half:].reshape(count // 2, -1, half)

    @pl.loop(1, count)
    def _(k):
        scatter(k, cross_part, cross_land, send_c, recv_c).start()

    cross_land[0] = cross_part[me]
    own = exact_parts(jnp.concatenate([state[0].T, state[1].T], axis=1))
    for which in range(2):

        @pl.loop(0, per_half)
        def _(step, which=which):
            wide = exact_dot(packed[which][rows_of(step), :], own)
            step = which * per_half + step
            out[rows_of(step), :] = mask_halves(wide, odd_rows(step, charge))

    store = pltpu.make_async_copy(out, out_hbm, store_sem)
    store.start()

    @pl.loop(1, count)
    def _(k):
        scatter(k, cross_part, cross_land, send_c, recv_c).wait_recv()

    cross_all[me] = jnp.sum(cross_land[...], axis=0)

    @pl.loop(1, count)
    def _(k):
        gather(k, me, cross_all, send_d, recv_d).start()

    inverse_down.wait_recv()
    following = exact_parts(jnp.concatenate([inverse_next[0].T, inverse_next[1].T], axis=1))
    next_rows = packed_next.reshape(phys, bond, half)
    spot = lax.broadcasted_iota(jnp.int32, (block, half), 0)

    @pl.loop(0, bond // group)
    def _(step):
        left = pl.ds(pl.multiple_of(step * group, group), group)
        rows = jnp.swapaxes(next_rows[:, left, :].astype(jnp.float32), 0, 1).reshape(block, half)
        odd = ((step * group + spot // phys) >= charge_above) != (lax.rem(spot, phys) >= phys // 2)
        wide = exact_dot(rows.astype(jnp.bfloat16), following)
        compressed_next[pl.ds(pl.multiple_of(step * block, block), block), :] = mask_halves(wide, odd)

    @pl.loop(1, count)
    def _(k):
        gather(k, before(k), cross_all, send_d, recv_d).wait_recv()

    total = jnp.concatenate(
        [cross_all[: count // 2].reshape(bond, half), cross_all[count // 2 :].reshape(bond, half)], axis=1
    )
    upper = jnp.concatenate(
        [
            jnp.dot(state[0], total[:half], precision=HIGH, preferred_element_type=jnp.float32),
            jnp.dot(state[1], total[half:], precision=HIGH, preferred_element_type=jnp.float32),
        ],
        axis=0,
    )
    turn = (((1,), (1,)), ((), ()))
    correlation = jnp.concatenate(
        [
            lax.dot_general(upper[:, :half], inverse_next[0], turn, precision=HIGH, preferred_element_type=jnp.float32),
            lax.dot_general(upper[:, half:], inverse_next[1], turn, precision=HIGH, preferred_element_type=jnp.float32),
        ],
        axis=1,
    )
    mixing = (correlation * mix_scale).T.astype(jnp.bfloat16)

    for step in range(pieces):
        mixed = jnp.dot(compressed_next[step * piece : (step + 1) * piece, :], mixing, preferred_element_type=jnp.float32)
        mixed = mixed.astype(jnp.bfloat16)
        for part in range(piece // block):
            column = (step * (piece // block) + part) * bond
            adjoints[:, column : column + bond] = mixed[part * block : (part + 1) * block]
    pairs = jnp.dot(adjoints[...], ordered[...], preferred_element_type=jnp.float32)
    down = lax.broadcasted_iota(jnp.int32, (block, block), 0)
    across = lax.broadcasted_iota(jnp.int32, (block, block), 1)
    pairs = jnp.where(down // phys == across // phys, pairs, 0.0).reshape(group, phys, block).sum(axis=0)
    tall = lax.broadcasted_iota(jnp.int32, (block, phys), 0)
    wide = lax.broadcasted_iota(jnp.int32, (block, phys), 1)
    fold = jnp.where(lax.rem(tall, phys) == wide, 1.0, 0.0)
    gradient = jnp.dot(pairs, fold, precision=HIGH, preferred_element_type=jnp.float32)
    grad_ref[...] = jnp.where(row == sections - 1, 0.0, gradient / bond)
    for copy in rows_down:
        copy.wait_send()
    charge_down.wait_send()
    inverse_down.wait_send()
    store.wait()

    @pl.loop(1, count)
    def _(k):
        scatter(k, gram_part, gram_land, send_a, recv_a).wait_send()
        gather(k, me, gram_all, send_b, recv_b).wait_send()
        scatter(k, cross_part, cross_land, send_c, recv_c).wait_send()
        gather(k, me, cross_all, send_d, recv_d).wait_send()


def shards(boundary_in, row_operator, charges):
    stored, oper, charge = boundary_in[0, 0], row_operator[0, 0], charges[0, 0]
    phys, bond = stored.shape[0], stored.shape[2]
    half, phalf = bond // 2, phys // 2
    count, sections = lax.axis_size("cols"), lax.axis_size("rows")
    left_odd = (jnp.arange(bond) >= charge)[None, :, None]
    low, high = stored[:, :, :half], stored[:, :, half:]
    even = jnp.einsum("pq,qlc->plc", oper[:phalf], jnp.where(left_odd, high, low), preferred_element_type=jnp.float32)
    other = jnp.einsum("pq,qlc->plc", oper[phalf:], jnp.where(left_odd, low, high), preferred_element_type=jnp.float32)
    even = even.astype(jnp.bfloat16).reshape(-1, half)
    other = other.astype(jnp.bfloat16).reshape(-1, half)
    scale = 2.0 / (count * phys * bond)
    mix_scale = 2.0 / (bond * math.sqrt(count * phys))
    vmem = pl.BlockSpec(memory_space=pltpu.VMEM)
    gram_shape = (count, half * bond // count // half, half)
    cross_shape = (count, bond * bond // count // half, half)
    sems = pltpu.SemaphoreType.DMA((count,))
    compressed, gradient = pl.pallas_call(
        functools.partial(whole_kernel, count, sections, phys, bond, scale, mix_scale),
        out_shape=(
            jax.ShapeDtypeStruct((phys * bond, bond), jnp.bfloat16),
            jax.ShapeDtypeStruct((phys, phys), jnp.float32),
        ),
        in_specs=[vmem, vmem, pl.BlockSpec(memory_space=pl.ANY), pl.BlockSpec(memory_space=pltpu.SMEM)],
        out_specs=(pl.BlockSpec(memory_space=pl.ANY), vmem),
        scratch_shapes=[
            pltpu.VMEM((phys, bond, bond), jnp.bfloat16),
            pltpu.VMEM((phys * bond, bond), jnp.bfloat16),
            pltpu.VMEM((phys * bond, half), jnp.bfloat16),
            pltpu.VMEM((phys * bond, bond), jnp.bfloat16),
            pltpu.VMEM((bond, phys * bond), jnp.bfloat16),
            pltpu.VMEM((bond, phys * bond), jnp.bfloat16),
            pltpu.VMEM((phys * bond, bond), jnp.bfloat16),
            pltpu.VMEM((8, half), jnp.int32),
            pltpu.VMEM((8, half), jnp.int32),
            pltpu.VMEM((2, half, half), jnp.float32),
            pltpu.VMEM((2, half, half), jnp.float32),
            pltpu.VMEM(gram_shape, jnp.float32),
            pltpu.VMEM(gram_shape, jnp.float32),
            pltpu.VMEM(gram_shape, jnp.float32),
            pltpu.VMEM(cross_shape, jnp.float32),
            pltpu.VMEM(cross_shape, jnp.float32),
            pltpu.VMEM(cross_shape, jnp.float32),
            sems, sems, sems, sems, sems, sems, sems, sems,
            pltpu.SemaphoreType.DMA((6,)),
            pltpu.SemaphoreType.DMA((6,)),
            pltpu.SemaphoreType.DMA,
            pltpu.SemaphoreType.DMA,
        ],
        compiler_params=pltpu.CompilerParams(collective_id=0, has_side_effects=True),
        name="orthonormalise",
    )(even, other, stored, charges)
    return (compressed.reshape(boundary_in.shape), gradient[None, None])


def solution(mesh):
    return jax.shard_map(
        shards,
        mesh=mesh,
        in_specs=(
            P("rows", "cols", None, None, None),
            P("rows", "cols", None, None),
            P("rows", "cols"),
        ),
        out_specs=(P("rows", "cols", None, None, None), P("rows", "cols", None, None)),
        check_vma=False,
    )
```

```python
import functools
import math

import jax
import jax.numpy as jnp
from jax import lax
from jax.experimental import pallas as pl
from jax.experimental.pallas import tpu as pltpu
from jax.sharding import PartitionSpec as P

HIGH = lax.Precision.HIGHEST
MESH = pl.DeviceIdType.MESH


def split3(x):
    high = x.astype(jnp.bfloat16).astype(jnp.float32)
    rest = x - high
    mid = rest.astype(jnp.bfloat16).astype(jnp.float32)
    return high, mid, rest - mid


def invert_factor(state, size, first, last):
    step = 8
    blocks = range(state.shape[0])
    lane = lax.broadcasted_iota(jnp.int32, (step, size), 1)
    sub = lax.broadcasted_iota(jnp.int32, (step, size), 0)
    lane_all = lax.broadcasted_iota(jnp.int32, (size, size), 1)
    for base in range(first, last, step):
        stop = base + step
        own = (lane >= base) & (lane < stop)
        for b in blocks:
            rows = state[b, base:stop, :]
            columns = [jnp.broadcast_to(rows[:, base + k : base + k + 1], (step, size)) for k in range(step)]
            unit = jnp.where(lane == sub + base, 1.0, 0.0)
            pivots = jnp.ones((step, size), jnp.float32)
            for k in range(step):
                pivot = jnp.broadcast_to(columns[k][k : k + 1, :], (step, size))
                pivots = jnp.where(sub == k, pivot, pivots)
                factor = jnp.where(sub > k, columns[k] / pivot, 0.0)
                for later in range(k + 1, step):
                    columns[later] = columns[later] - factor * jnp.broadcast_to(columns[later][k : k + 1, :], (step, size))
                rows = rows - factor * jnp.broadcast_to(rows[k : k + 1, :], (step, size))
                unit = unit - factor * jnp.broadcast_to(unit[k : k + 1, :], (step, size))
            done = jnp.where(own, unit, rows)
            if stop < size:
                lh, lm, ll = split3(rows / pivots)
                rh, rm, rl = split3(done)
                left = jnp.concatenate([lh, lh, lm, lh, ll, lm], axis=0).astype(jnp.bfloat16)
                right = jnp.concatenate([rh, rm, rh, rl, rh, rm], axis=0).astype(jnp.bfloat16)
                update = lax.dot_general(left, right, (((0,), (0,)), ((), ())), preferred_element_type=jnp.float32)
                below = state[b, stop:, :]
                inside = (lane_all[stop:] >= base) & (lane_all[stop:] < stop)
                state[b, stop:, :] = jnp.where(inside, 0.0, below) - update[stop:]
            state[b, base:stop, :] = jnp.where(lane <= sub + base, done * lax.rsqrt(pivots), 0.0)


def exact_parts(weights):
    high, mid, low = split3(weights)
    return jnp.concatenate([high, mid], axis=0).astype(jnp.bfloat16), low.astype(jnp.bfloat16)


def exact_dot(rows, parts):
    out = jnp.dot(jnp.concatenate([rows, rows], axis=1), parts[0], preferred_element_type=jnp.float32)
    return out + jnp.dot(rows, parts[1], preferred_element_type=jnp.float32)


def unpack(rows, odd):
    wide = rows.astype(jnp.float32)
    return jnp.concatenate([jnp.where(odd, 0.0, wide), jnp.where(odd, wide, 0.0)], axis=1).astype(jnp.bfloat16)


def mask_halves(out, odd):
    half = out.shape[1] // 2
    return jnp.concatenate([jnp.where(odd, 0.0, out[:, :half]), jnp.where(odd, out[:, half:], 0.0)], axis=1).astype(jnp.bfloat16)


def whole_kernel(
    count, sections, phys, bond, scale, mix_scale,
    even_ref, other_ref, stored_hbm, charge_ref,
    out_hbm, grad_ref,
    stored, ordered, packed_next, compressed_next, turned, adjoints, out, charge_own, charge_next,
    state, inverse_next, gram_part, gram_land, gram_all, cross_part, cross_land, cross_all,
    send_a, recv_a, send_b, recv_b, send_c, recv_c, send_d, recv_d, send_r, recv_r, load_sem, store_sem,
):
    me = lax.axis_index("cols")
    row = lax.axis_index("rows")
    half = bond // 2
    below = lax.rem(row + sections - 1, sections)
    above = lax.rem(row + 1, sections)

    def after(k):
        return lax.rem(me + k, count)

    def before(k):
        return lax.rem(me + count - k, count)

    barrier = pltpu.get_barrier_semaphore()
    pl.semaphore_signal(barrier, inc=1, device_id={"rows": below}, device_id_type=MESH)
    pl.semaphore_signal(barrier, inc=1, device_id={"rows": above}, device_id_type=MESH)

    @pl.loop(1, count)
    def _(k):
        pl.semaphore_signal(barrier, inc=1, device_id={"cols": after(k)}, device_id_type=MESH)

    load = pltpu.make_async_copy(stored_hbm, stored, load_sem)
    load.start()
    charge = charge_ref[0, 0]
    charge_own[...] = jnp.full(charge_own.shape, charge, jnp.int32)
    tile = 2 * bond
    tiles = phys // 2
    place = lax.broadcasted_iota(jnp.int32, (tile, half), 0)

    phalf = phys // 2
    lefts = tile // phalf

    def odd_rows(which, step, charge):
        left_odd = (step * lefts + place // phalf) >= charge
        return left_odd != (which == 1)

    packed = (even_ref, other_ref)
    per_half = tiles // 2

    def rows_of(step):
        return pl.ds(pl.multiple_of(step * tile, tile), tile)

    def to_below(source, target, index):
        return pltpu.make_async_remote_copy(
            src_ref=source, dst_ref=target, send_sem=send_r.at[index], recv_sem=recv_r.at[index],
            device_id={"rows": below}, device_id_type=MESH,
        )

    pieces = 4
    piece = phys * bond // pieces
    charge_down = to_below(charge_own, charge_next, pieces)
    rows_down = []
    for index in range(pieces):
        start = index * piece % (pieces // 2 * piece)
        source = packed[index * 2 // pieces].at[start : start + piece, :]
        rows_down.append(to_below(source, packed_next.at[index * piece : (index + 1) * piece, :], index))
    pl.semaphore_wait(barrier, count + 1)
    charge_down.start()
    for copy in rows_down:
        copy.start()
    lane_place = lax.broadcasted_iota(jnp.int32, (half, tile), 1)
    gram = jnp.zeros((half, bond), jnp.float32)
    for which in range(2):

        def gram_step(step, total, which=which):
            rows = packed[which][rows_of(step), :]
            across = rows.T
            flat = unpack(rows, odd_rows(which, step, charge))
            wide = across.astype(jnp.float32)
            odd = ((step * lefts + lane_place // phalf) >= charge) != (which == 1)
            columns = rows_of(which * per_half + step)
            turned[:half, columns] = jnp.where(odd, 0.0, wide).astype(jnp.bfloat16)
            turned[half:, columns] = jnp.where(odd, wide, 0.0).astype(jnp.bfloat16)
            return total + jnp.dot(across, flat, preferred_element_type=jnp.float32)

        gram = lax.fori_loop(0, per_half, gram_step, gram)
    gram_part[: count // 2] = gram[:, :half].reshape(count // 2, -1, half)
    gram_part[count // 2 :] = gram[:, half:].reshape(count // 2, -1, half)

    def scatter(k, part, land, send, recv):
        return pltpu.make_async_remote_copy(
            src_ref=part.at[after(k)], dst_ref=land.at[k], send_sem=send.at[k], recv_sem=recv.at[k],
            device_id={"cols": after(k)}, device_id_type=MESH,
        )

    def gather(k, owner, whole, send, recv):
        return pltpu.make_async_remote_copy(
            src_ref=whole.at[owner], dst_ref=whole.at[owner], send_sem=send.at[k], recv_sem=recv.at[k],
            device_id={"cols": after(k)}, device_id_type=MESH,
        )

    @pl.loop(1, count)
    def _(k):
        scatter(k, gram_part, gram_land, send_a, recv_a).start()

    gram_land[0] = gram_part[me]
    load.wait()
    group = bond // phys
    block = group * phys

    def reorder(step, source, target):
        left = pl.ds(pl.multiple_of(step * group, group), group)
        rows = source[:, left, :].astype(jnp.float32)
        rows = jnp.swapaxes(rows, 0, 1).reshape(block, rows.shape[2])
        target[pl.ds(pl.multiple_of(step * bond, bond), bond), :] = rows.T.astype(jnp.bfloat16)

    @pl.loop(0, bond // group // 2)
    def _(step):
        reorder(step, stored, ordered)

    @pl.loop(1, count)
    def _(k):
        scatter(k, gram_part, gram_land, send_a, recv_a).wait_recv()

    gram_all[me] = jnp.sum(gram_land[...], axis=0)

    @pl.loop(1, count)
    def _(k):
        gather(k, me, gram_all, send_b, recv_b).start()

    @pl.loop(bond // group // 2, bond // group)
    def _(step):
        reorder(step, stored, ordered)

    @pl.loop(1, count)
    def _(k):
        gather(k, before(k), gram_all, send_b, recv_b).wait_recv()

    state[0] = gram_all[: count // 2].reshape(half, half) * scale
    state[1] = gram_all[count // 2 :].reshape(half, half) * scale
    invert_factor(state, half, 0, half)
    inverse_down = to_below(state, inverse_next, pieces + 1)
    inverse_down.start()
    charge_down.wait_recv()
    charge_above = charge_next[0:1, :]
    cross = jnp.zeros((bond, bond), jnp.float32)
    for index in range(pieces):
        rows_down[index].wait_recv()
        first = index * piece // tile
        other = jnp.concatenate(
            [
                unpack(packed_next[step * tile : (step + 1) * tile, :], odd_rows(step // per_half, step % per_half, charge_above))
                for step in range(first, first + piece // tile)
            ],
            axis=0,
        )
        cross += jnp.dot(turned[:, index * piece : (index + 1) * piece], other, preferred_element_type=jnp.float32)
    cross_part[: count // 2] = cross[:, :half].reshape(count // 2, -1, half)
    cross_part[count // 2 :] = cross[:, half:].reshape(count // 2, -1, half)

    @pl.loop(1, count)
    def _(k):
        scatter(k, cross_part, cross_land, send_c, recv_c).start()

    cross_land[0] = cross_part[me]
    own = exact_parts(jnp.concatenate([state[0].T, state[1].T], axis=1))
    for which in range(2):

        @pl.loop(0, per_half)
        def _(step, which=which):
            wide = exact_dot(packed[which][rows_of(step), :], own)
            wide = mask_halves(wide, odd_rows(which, step, charge)).astype(jnp.float32)
            wide = jnp.swapaxes(wide.reshape(lefts, phalf, bond), 0, 1)
            left = pl.ds(pl.multiple_of(step * lefts, lefts), lefts)
            out[which * phalf : (which + 1) * phalf, left, :] = wide.astype(jnp.bfloat16)

    store = pltpu.make_async_copy(out, out_hbm, store_sem)
    store.start()

    @pl.loop(1, count)
    def _(k):
        scatter(k, cross_part, cross_land, send_c, recv_c).wait_recv()

    cross_all[me] = jnp.sum(cross_land[...], axis=0)

    @pl.loop(1, count)
    def _(k):
        gather(k, me, cross_all, send_d, recv_d).start()

    inverse_down.wait_recv()
    following = exact_parts(jnp.concatenate([inverse_next[0].T, inverse_next[1].T], axis=1))
    for which in range(2):

        @pl.loop(0, per_half)
        def _(step, which=which):
            rows = rows_of(which * per_half + step)
            wide = exact_dot(packed_next[rows, :], following)
            compressed_next[rows, :] = mask_halves(wide, odd_rows(which, step, charge_above))

    @pl.loop(1, count)
    def _(k):
        gather(k, before(k), cross_all, send_d, recv_d).wait_recv()

    total = jnp.concatenate(
        [cross_all[: count // 2].reshape(bond, half), cross_all[count // 2 :].reshape(bond, half)], axis=1
    )
    upper = jnp.concatenate(
        [
            jnp.dot(state[0], total[:half], precision=HIGH, preferred_element_type=jnp.float32),
            jnp.dot(state[1], total[half:], precision=HIGH, preferred_element_type=jnp.float32),
        ],
        axis=0,
    )
    turn = (((1,), (1,)), ((), ()))
    correlation = jnp.concatenate(
        [
            lax.dot_general(upper[:, :half], inverse_next[0], turn, precision=HIGH, preferred_element_type=jnp.float32),
            lax.dot_general(upper[:, half:], inverse_next[1], turn, precision=HIGH, preferred_element_type=jnp.float32),
        ],
        axis=1,
    )
    mixing = (correlation * mix_scale).T.astype(jnp.bfloat16)

    for step in range(pieces):
        mixed = jnp.dot(compressed_next[step * piece : (step + 1) * piece, :], mixing, preferred_element_type=jnp.float32)
        mixed = mixed.astype(jnp.bfloat16)
        which, place_in_half = divmod(step, pieces // 2)
        height = block // 2
        for part in range(piece // height):
            column = (place_in_half * (piece // height) + part) * bond
            chunk = mixed[part * height : (part + 1) * height]
            adjoints[which * height : (which + 1) * height, column : column + bond] = chunk
    pairs = jnp.dot(adjoints[...], ordered[...], preferred_element_type=jnp.float32)
    down = lax.broadcasted_iota(jnp.int32, (block, block), 0)
    across = lax.broadcasted_iota(jnp.int32, (block, block), 1)
    same = lax.rem(down, block // 2) // phalf == across // phys
    pairs = jnp.where(same, pairs, 0.0).reshape(2, group, phalf, block).sum(axis=1).reshape(phys, block)
    tall = lax.broadcasted_iota(jnp.int32, (block, phys), 0)
    wide = lax.broadcasted_iota(jnp.int32, (block, phys), 1)
    fold = jnp.where(lax.rem(tall, phys) == wide, 1.0, 0.0)
    gradient = jnp.dot(pairs, fold, precision=HIGH, preferred_element_type=jnp.float32)
    grad_ref[...] = jnp.where(row == sections - 1, 0.0, gradient / bond)
    for copy in rows_down:
        copy.wait_send()
    charge_down.wait_send()
    inverse_down.wait_send()
    store.wait()

    @pl.loop(1, count)
    def _(k):
        scatter(k, gram_part, gram_land, send_a, recv_a).wait_send()
        gather(k, me, gram_all, send_b, recv_b).wait_send()
        scatter(k, cross_part, cross_land, send_c, recv_c).wait_send()
        gather(k, me, cross_all, send_d, recv_d).wait_send()


def shards(boundary_in, row_operator, charges):
    stored, oper, charge = boundary_in[0, 0], row_operator[0, 0], charges[0, 0]
    phys, bond = stored.shape[0], stored.shape[2]
    half, phalf = bond // 2, phys // 2
    count, sections = lax.axis_size("cols"), lax.axis_size("rows")
    left_odd = (jnp.arange(bond) >= charge)[None, :, None]
    low, high = stored[:, :, :half], stored[:, :, half:]
    even = jnp.einsum("pq,qlc->lpc", oper[:phalf], jnp.where(left_odd, high, low), preferred_element_type=jnp.float32)
    other = jnp.einsum("pq,qlc->lpc", oper[phalf:], jnp.where(left_odd, low, high), preferred_element_type=jnp.float32)
    even = even.astype(jnp.bfloat16).reshape(-1, half)
    other = other.astype(jnp.bfloat16).reshape(-1, half)
    scale = 2.0 / (count * phys * bond)
    mix_scale = 2.0 / (bond * math.sqrt(count * phys))
    vmem = pl.BlockSpec(memory_space=pltpu.VMEM)
    gram_shape = (count, half * bond // count // half, half)
    cross_shape = (count, bond * bond // count // half, half)
    sems = pltpu.SemaphoreType.DMA((count,))
    compressed, gradient = pl.pallas_call(
        functools.partial(whole_kernel, count, sections, phys, bond, scale, mix_scale),
        out_shape=(
            jax.ShapeDtypeStruct((phys, bond, bond), jnp.bfloat16),
            jax.ShapeDtypeStruct((phys, phys), jnp.float32),
        ),
        in_specs=[vmem, vmem, pl.BlockSpec(memory_space=pl.ANY), pl.BlockSpec(memory_space=pltpu.SMEM)],
        out_specs=(pl.BlockSpec(memory_space=pl.ANY), vmem),
        scratch_shapes=[
            pltpu.VMEM((phys, bond, bond), jnp.bfloat16),
            pltpu.VMEM((phys * bond, bond), jnp.bfloat16),
            pltpu.VMEM((phys * bond, half), jnp.bfloat16),
            pltpu.VMEM((phys * bond, bond), jnp.bfloat16),
            pltpu.VMEM((bond, phys * bond), jnp.bfloat16),
            pltpu.VMEM((bond, phys * bond), jnp.bfloat16),
            pltpu.VMEM((phys, bond, bond), jnp.bfloat16),
            pltpu.VMEM((8, half), jnp.int32),
            pltpu.VMEM((8, half), jnp.int32),
            pltpu.VMEM((2, half, half), jnp.float32),
            pltpu.VMEM((2, half, half), jnp.float32),
            pltpu.VMEM(gram_shape, jnp.float32),
            pltpu.VMEM(gram_shape, jnp.float32),
            pltpu.VMEM(gram_shape, jnp.float32),
            pltpu.VMEM(cross_shape, jnp.float32),
            pltpu.VMEM(cross_shape, jnp.float32),
            pltpu.VMEM(cross_shape, jnp.float32),
            sems, sems, sems, sems, sems, sems, sems, sems,
            pltpu.SemaphoreType.DMA((6,)),
            pltpu.SemaphoreType.DMA((6,)),
            pltpu.SemaphoreType.DMA,
            pltpu.SemaphoreType.DMA,
        ],
        compiler_params=pltpu.CompilerParams(collective_id=0, has_side_effects=True),
        name="orthonormalise",
    )(even, other, stored, charges)
    return (compressed.reshape(boundary_in.shape), gradient[None, None])


def solution(mesh):
    return jax.shard_map(
        shards,
        mesh=mesh,
        in_specs=(
            P("rows", "cols", None, None, None),
            P("rows", "cols", None, None),
            P("rows", "cols"),
        ),
        out_specs=(P("rows", "cols", None, None, None), P("rows", "cols", None, None)),
        check_vma=False,
    )
```

```python
import functools
import math

import jax
import jax.numpy as jnp
from jax import lax
from jax.experimental import pallas as pl
from jax.experimental.pallas import tpu as pltpu
from jax.sharding import PartitionSpec as P

HIGH = lax.Precision.HIGHEST
MESH = pl.DeviceIdType.MESH


def split3(x):
    high = x.astype(jnp.bfloat16).astype(jnp.float32)
    rest = x - high
    mid = rest.astype(jnp.bfloat16).astype(jnp.float32)
    return high, mid, rest - mid


def invert_factor(state, size, first, last):
    step = 8
    blocks = range(state.shape[0])
    lane = lax.broadcasted_iota(jnp.int32, (step, size), 1)
    sub = lax.broadcasted_iota(jnp.int32, (step, size), 0)
    lane_all = lax.broadcasted_iota(jnp.int32, (size, size), 1)
    for base in range(first, last, step):
        stop = base + step
        own = (lane >= base) & (lane < stop)
        for b in blocks:
            rows = state[b, base:stop, :]
            columns = [jnp.broadcast_to(rows[:, base + k : base + k + 1], (step, size)) for k in range(step)]
            unit = jnp.where(lane == sub + base, 1.0, 0.0)
            pivots = jnp.ones((step, size), jnp.float32)
            for k in range(step):
                pivot = jnp.broadcast_to(columns[k][k : k + 1, :], (step, size))
                pivots = jnp.where(sub == k, pivot, pivots)
                factor = jnp.where(sub > k, columns[k] / pivot, 0.0)
                for later in range(k + 1, step):
                    columns[later] = columns[later] - factor * jnp.broadcast_to(columns[later][k : k + 1, :], (step, size))
                rows = rows - factor * jnp.broadcast_to(rows[k : k + 1, :], (step, size))
                unit = unit - factor * jnp.broadcast_to(unit[k : k + 1, :], (step, size))
            done = jnp.where(own, unit, rows)
            if stop < size:
                lh, lm, ll = split3(rows / pivots)
                rh, rm, rl = split3(done)
                left = jnp.concatenate([lh, lh, lm, lh, ll, lm], axis=0).astype(jnp.bfloat16)
                right = jnp.concatenate([rh, rm, rh, rl, rh, rm], axis=0).astype(jnp.bfloat16)
                update = lax.dot_general(left, right, (((0,), (0,)), ((), ())), preferred_element_type=jnp.float32)
                below = state[b, stop:, :]
                inside = (lane_all[stop:] >= base) & (lane_all[stop:] < stop)
                state[b, stop:, :] = jnp.where(inside, 0.0, below) - update[stop:]
            state[b, base:stop, :] = jnp.where(lane <= sub + base, done * lax.rsqrt(pivots), 0.0)


def exact_parts(weights):
    high, mid, low = split3(weights)
    return jnp.concatenate([high, mid], axis=0).astype(jnp.bfloat16), low.astype(jnp.bfloat16)


def exact_dot(rows, parts):
    out = jnp.dot(jnp.concatenate([rows, rows], axis=1), parts[0], preferred_element_type=jnp.float32)
    return out + jnp.dot(rows, parts[1], preferred_element_type=jnp.float32)


def unpack(rows, odd):
    wide = rows.astype(jnp.float32)
    return jnp.concatenate([jnp.where(odd, 0.0, wide), jnp.where(odd, wide, 0.0)], axis=1).astype(jnp.bfloat16)


def mask_halves(out, odd):
    half = out.shape[1] // 2
    return jnp.concatenate([jnp.where(odd, 0.0, out[:, :half]), jnp.where(odd, out[:, half:], 0.0)], axis=1).astype(jnp.bfloat16)


def spread_kernel(steps, charge_ref, rows_ref, pairs_ref, out_ref, grad_ref):
    half = rows_ref.shape[2]
    phys_odd = (pl.program_id(0) >= steps).astype(jnp.int32)
    left_odd = (lax.broadcasted_iota(jnp.int32, rows_ref.shape, 1) >= charge_ref[0, 0]).astype(jnp.int32)
    odd = left_odd != phys_odd
    rows = rows_ref[...].astype(jnp.float32)
    out_ref[:, :, :half] = jnp.where(odd, 0.0, rows).astype(jnp.bfloat16)
    out_ref[:, :, half:] = jnp.where(odd, rows, 0.0).astype(jnp.bfloat16)
    grad_ref[...] = pairs_ref[...]


def whole_kernel(
    count, sections, phys, bond, scale, mix_scale,
    even_ref, other_ref, stored_hbm, charge_ref,
    out_hbm, grad_ref,
    stored, ordered, packed_next, compressed_next, turned, adjoints, out, charge_own, charge_next,
    state, inverse_next, gram_part, gram_land, gram_all, cross_part, cross_land, cross_all,
    send_a, recv_a, send_b, recv_b, send_c, recv_c, send_d, recv_d, send_r, recv_r, load_sem, store_sem,
):
    me = lax.axis_index("cols")
    row = lax.axis_index("rows")
    half = bond // 2
    below = lax.rem(row + sections - 1, sections)
    above = lax.rem(row + 1, sections)

    def after(k):
        return lax.rem(me + k, count)

    def before(k):
        return lax.rem(me + count - k, count)

    barrier = pltpu.get_barrier_semaphore()
    pl.semaphore_signal(barrier, inc=1, device_id={"rows": below}, device_id_type=MESH)
    pl.semaphore_signal(barrier, inc=1, device_id={"rows": above}, device_id_type=MESH)

    @pl.loop(1, count)
    def _(k):
        pl.semaphore_signal(barrier, inc=1, device_id={"cols": after(k)}, device_id_type=MESH)

    load = pltpu.make_async_copy(stored_hbm, stored, load_sem)
    load.start()
    charge = charge_ref[0, 0]
    charge_own[...] = jnp.full(charge_own.shape, charge, jnp.int32)
    tile = 2 * bond
    tiles = phys // 2
    place = lax.broadcasted_iota(jnp.int32, (tile, half), 0)

    phalf = phys // 2
    lefts = tile // phalf

    def odd_rows(which, step, charge):
        left_odd = (step * lefts + place // phalf) >= charge
        return left_odd != (which == 1)

    packed = (even_ref, other_ref)
    per_half = tiles // 2

    def rows_of(step):
        return pl.ds(pl.multiple_of(step * tile, tile), tile)

    def to_below(source, target, index):
        return pltpu.make_async_remote_copy(
            src_ref=source, dst_ref=target, send_sem=send_r.at[index], recv_sem=recv_r.at[index],
            device_id={"rows": below}, device_id_type=MESH,
        )

    pieces = 4
    piece = phys * bond // pieces
    charge_down = to_below(charge_own, charge_next, pieces)
    rows_down = []
    for index in range(pieces):
        start = index * piece % (pieces // 2 * piece)
        source = packed[index * 2 // pieces].at[start : start + piece, :]
        rows_down.append(to_below(source, packed_next.at[index * piece : (index + 1) * piece, :], index))
    pl.semaphore_wait(barrier, count + 1)
    charge_down.start()
    for copy in rows_down:
        copy.start()
    lane_place = lax.broadcasted_iota(jnp.int32, (half, tile), 1)
    gram = jnp.zeros((half, bond), jnp.float32)
    for which in range(2):

        def gram_step(step, total, which=which):
            rows = packed[which][rows_of(step), :]
            across = rows.T
            flat = unpack(rows, odd_rows(which, step, charge))
            wide = across.astype(jnp.float32)
            odd = ((step * lefts + lane_place // phalf) >= charge) != (which == 1)
            columns = rows_of(which * per_half + step)
            turned[:half, columns] = jnp.where(odd, 0.0, wide).astype(jnp.bfloat16)
            turned[half:, columns] = jnp.where(odd, wide, 0.0).astype(jnp.bfloat16)
            return total + jnp.dot(across, flat, preferred_element_type=jnp.float32)

        gram = lax.fori_loop(0, per_half, gram_step, gram)
    gram_part[: count // 2] = gram[:, :half].reshape(count // 2, -1, half)
    gram_part[count // 2 :] = gram[:, half:].reshape(count // 2, -1, half)

    def scatter(k, part, land, send, recv):
        return pltpu.make_async_remote_copy(
            src_ref=part.at[after(k)], dst_ref=land.at[k], send_sem=send.at[k], recv_sem=recv.at[k],
            device_id={"cols": after(k)}, device_id_type=MESH,
        )

    def gather(k, owner, whole, send, recv):
        return pltpu.make_async_remote_copy(
            src_ref=whole.at[owner], dst_ref=whole.at[owner], send_sem=send.at[k], recv_sem=recv.at[k],
            device_id={"cols": after(k)}, device_id_type=MESH,
        )

    @pl.loop(1, count)
    def _(k):
        scatter(k, gram_part, gram_land, send_a, recv_a).start()

    gram_land[0] = gram_part[me]
    load.wait()
    group = bond // phys
    block = group * phys

    def reorder(step, source, target):
        left = pl.ds(pl.multiple_of(step * group, group), group)
        rows = source[:, left, :].astype(jnp.float32)
        rows = jnp.swapaxes(rows, 0, 1).reshape(block, rows.shape[2])
        target[pl.ds(pl.multiple_of(step * bond, bond), bond), :] = rows.T.astype(jnp.bfloat16)

    @pl.loop(0, bond // group // 2)
    def _(step):
        reorder(step, stored, ordered)

    @pl.loop(1, count)
    def _(k):
        scatter(k, gram_part, gram_land, send_a, recv_a).wait_recv()

    gram_all[me] = jnp.sum(gram_land[...], axis=0)

    @pl.loop(1, count)
    def _(k):
        gather(k, me, gram_all, send_b, recv_b).start()

    @pl.loop(bond // group // 2, bond // group)
    def _(step):
        reorder(step, stored, ordered)

    @pl.loop(1, count)
    def _(k):
        gather(k, before(k), gram_all, send_b, recv_b).wait_recv()

    state[0] = gram_all[: count // 2].reshape(half, half) * scale
    state[1] = gram_all[count // 2 :].reshape(half, half) * scale
    invert_factor(state, half, 0, half)
    inverse_down = to_below(state, inverse_next, pieces + 1)
    inverse_down.start()
    own = exact_parts(jnp.concatenate([state[0].T, state[1].T], axis=1))

    def compress_half(which):
        @pl.loop(0, per_half)
        def _(step):
            wide = exact_dot(packed[which][rows_of(step), :], own)
            wide = jnp.where(odd_rows(which, step, charge), wide[:, half:], wide[:, :half])
            wide = jnp.swapaxes(wide.reshape(lefts, phalf, half), 0, 1)
            left = pl.ds(pl.multiple_of(step * lefts, lefts), lefts)
            out[which * phalf : (which + 1) * phalf, left, :] = wide.astype(jnp.bfloat16)

    compress_half(0)
    charge_down.wait_recv()
    charge_above = charge_next[0:1, :]
    cross = jnp.zeros((bond, bond), jnp.float32)
    for index in range(pieces):
        rows_down[index].wait_recv()
        first = index * piece // tile
        other = jnp.concatenate(
            [
                unpack(packed_next[step * tile : (step + 1) * tile, :], odd_rows(step // per_half, step % per_half, charge_above))
                for step in range(first, first + piece // tile)
            ],
            axis=0,
        )
        cross += jnp.dot(turned[:, index * piece : (index + 1) * piece], other, preferred_element_type=jnp.float32)
    cross_part[: count // 2] = cross[:, :half].reshape(count // 2, -1, half)
    cross_part[count // 2 :] = cross[:, half:].reshape(count // 2, -1, half)

    @pl.loop(1, count)
    def _(k):
        scatter(k, cross_part, cross_land, send_c, recv_c).start()

    cross_land[0] = cross_part[me]
    compress_half(1)
    store = pltpu.make_async_copy(out, out_hbm, store_sem)
    store.start()

    @pl.loop(1, count)
    def _(k):
        scatter(k, cross_part, cross_land, send_c, recv_c).wait_recv()

    cross_all[me] = jnp.sum(cross_land[...], axis=0)

    @pl.loop(1, count)
    def _(k):
        gather(k, me, cross_all, send_d, recv_d).start()

    inverse_down.wait_recv()
    following = exact_parts(jnp.concatenate([inverse_next[0].T, inverse_next[1].T], axis=1))
    for which in range(2):

        @pl.loop(0, per_half)
        def _(step, which=which):
            rows = rows_of(which * per_half + step)
            wide = exact_dot(packed_next[rows, :], following)
            compressed_next[rows, :] = mask_halves(wide, odd_rows(which, step, charge_above))

    @pl.loop(1, count)
    def _(k):
        gather(k, before(k), cross_all, send_d, recv_d).wait_recv()

    total = jnp.concatenate(
        [cross_all[: count // 2].reshape(bond, half), cross_all[count // 2 :].reshape(bond, half)], axis=1
    )
    upper = jnp.concatenate(
        [
            jnp.dot(state[0], total[:half], precision=HIGH, preferred_element_type=jnp.float32),
            jnp.dot(state[1], total[half:], precision=HIGH, preferred_element_type=jnp.float32),
        ],
        axis=0,
    )
    turn = (((1,), (1,)), ((), ()))
    correlation = jnp.concatenate(
        [
            lax.dot_general(upper[:, :half], inverse_next[0], turn, precision=HIGH, preferred_element_type=jnp.float32),
            lax.dot_general(upper[:, half:], inverse_next[1], turn, precision=HIGH, preferred_element_type=jnp.float32),
        ],
        axis=1,
    )
    mixing = (correlation * mix_scale).T.astype(jnp.bfloat16)

    for step in range(pieces):
        mixed = jnp.dot(compressed_next[step * piece : (step + 1) * piece, :], mixing, preferred_element_type=jnp.float32)
        mixed = mixed.astype(jnp.bfloat16)
        which, place_in_half = divmod(step, pieces // 2)
        height = block // 2
        for part in range(piece // height):
            column = (place_in_half * (piece // height) + part) * bond
            chunk = mixed[part * height : (part + 1) * height]
            adjoints[which * height : (which + 1) * height, column : column + bond] = chunk
    pairs = jnp.dot(adjoints[...], ordered[...], preferred_element_type=jnp.float32)
    down = lax.broadcasted_iota(jnp.int32, (block, block), 0)
    across = lax.broadcasted_iota(jnp.int32, (block, block), 1)
    same = lax.rem(down, block // 2) // phalf == across // phys
    pairs = jnp.where(same, pairs, 0.0).reshape(2, group, phalf, block).sum(axis=1).reshape(phys, block)
    tall = lax.broadcasted_iota(jnp.int32, (block, phys), 0)
    wide = lax.broadcasted_iota(jnp.int32, (block, phys), 1)
    fold = jnp.where(lax.rem(tall, phys) == wide, 1.0, 0.0)
    gradient = jnp.dot(pairs, fold, precision=HIGH, preferred_element_type=jnp.float32)
    grad_ref[...] = jnp.where(row == sections - 1, 0.0, gradient / bond)
    for copy in rows_down:
        copy.wait_send()
    charge_down.wait_send()
    inverse_down.wait_send()
    store.wait()

    @pl.loop(1, count)
    def _(k):
        scatter(k, gram_part, gram_land, send_a, recv_a).wait_send()
        gather(k, me, gram_all, send_b, recv_b).wait_send()
        scatter(k, cross_part, cross_land, send_c, recv_c).wait_send()
        gather(k, me, cross_all, send_d, recv_d).wait_send()


def shards(boundary_in, row_operator, charges):
    stored, oper, charge = boundary_in[0, 0], row_operator[0, 0], charges[0, 0]
    phys, bond = stored.shape[0], stored.shape[2]
    half, phalf = bond // 2, phys // 2
    count, sections = lax.axis_size("cols"), lax.axis_size("rows")
    left_odd = (jnp.arange(bond) >= charge)[None, :, None]
    low, high = stored[:, :, :half], stored[:, :, half:]
    even = jnp.einsum("pq,qlc->lpc", oper[:phalf], jnp.where(left_odd, high, low), preferred_element_type=jnp.float32)
    other = jnp.einsum("pq,qlc->lpc", oper[phalf:], jnp.where(left_odd, low, high), preferred_element_type=jnp.float32)
    even = even.astype(jnp.bfloat16).reshape(-1, half)
    other = other.astype(jnp.bfloat16).reshape(-1, half)
    scale = 2.0 / (count * phys * bond)
    mix_scale = 2.0 / (bond * math.sqrt(count * phys))
    vmem = pl.BlockSpec(memory_space=pltpu.VMEM)
    gram_shape = (count, half * bond // count // half, half)
    cross_shape = (count, bond * bond // count // half, half)
    sems = pltpu.SemaphoreType.DMA((count,))
    compressed, gradient = pl.pallas_call(
        functools.partial(whole_kernel, count, sections, phys, bond, scale, mix_scale),
        out_shape=(
            jax.ShapeDtypeStruct((phys, bond, half), jnp.bfloat16),
            jax.ShapeDtypeStruct((phys, phys), jnp.float32),
        ),
        in_specs=[vmem, vmem, pl.BlockSpec(memory_space=pl.ANY), pl.BlockSpec(memory_space=pltpu.SMEM)],
        out_specs=(pl.BlockSpec(memory_space=pl.ANY), vmem),
        scratch_shapes=[
            pltpu.VMEM((phys, bond, bond), jnp.bfloat16),
            pltpu.VMEM((phys * bond, bond), jnp.bfloat16),
            pltpu.VMEM((phys * bond, half), jnp.bfloat16),
            pltpu.VMEM((phys * bond, bond), jnp.bfloat16),
            pltpu.VMEM((bond, phys * bond), jnp.bfloat16),
            pltpu.VMEM((bond, phys * bond), jnp.bfloat16),
            pltpu.VMEM((phys, bond, half), jnp.bfloat16),
            pltpu.VMEM((8, half), jnp.int32),
            pltpu.VMEM((8, half), jnp.int32),
            pltpu.VMEM((2, half, half), jnp.float32),
            pltpu.VMEM((2, half, half), jnp.float32),
            pltpu.VMEM(gram_shape, jnp.float32),
            pltpu.VMEM(gram_shape, jnp.float32),
            pltpu.VMEM(gram_shape, jnp.float32),
            pltpu.VMEM(cross_shape, jnp.float32),
            pltpu.VMEM(cross_shape, jnp.float32),
            pltpu.VMEM(cross_shape, jnp.float32),
            sems, sems, sems, sems, sems, sems, sems, sems,
            pltpu.SemaphoreType.DMA((6,)),
            pltpu.SemaphoreType.DMA((6,)),
            pltpu.SemaphoreType.DMA,
            pltpu.SemaphoreType.DMA,
        ],
        compiler_params=pltpu.CompilerParams(collective_id=0, has_side_effects=True),
        name="orthonormalise",
    )(even, other, stored, charges)
    spread = 4
    compressed, gradient = pl.pallas_call(
        functools.partial(spread_kernel, phalf // spread),
        grid=(phys // spread,),
        out_shape=(
            jax.ShapeDtypeStruct((phys, bond, bond), jnp.bfloat16),
            jax.ShapeDtypeStruct((phys, phys), jnp.float32),
        ),
        in_specs=[
            pl.BlockSpec(memory_space=pltpu.SMEM),
            pl.BlockSpec((spread, bond, half), lambda i: (i, 0, 0)),
            pl.BlockSpec((phys, phys), lambda i: (0, 0)),
        ],
        out_specs=(
            pl.BlockSpec((spread, bond, bond), lambda i: (i, 0, 0)),
            pl.BlockSpec((phys, phys), lambda i: (0, 0)),
        ),
        name="spread",
    )(charges, compressed, gradient)
    return (compressed.reshape(boundary_in.shape), gradient[None, None])


def solution(mesh):
    return jax.shard_map(
        shards,
        mesh=mesh,
        in_specs=(
            P("rows", "cols", None, None, None),
            P("rows", "cols", None, None),
            P("rows", "cols"),
        ),
        out_specs=(P("rows", "cols", None, None, None), P("rows", "cols", None, None)),
        check_vma=False,
    )
```

```python
import functools
import math

import jax
import jax.numpy as jnp
from jax import lax
from jax.experimental import pallas as pl
from jax.experimental.pallas import tpu as pltpu
from jax.sharding import PartitionSpec as P

HIGH = lax.Precision.HIGHEST
MESH = pl.DeviceIdType.MESH


def split3(x):
    high = x.astype(jnp.bfloat16).astype(jnp.float32)
    rest = x - high
    mid = rest.astype(jnp.bfloat16).astype(jnp.float32)
    return high, mid, rest - mid


def invert_factor(state, size, first, last):
    step = 8
    blocks = range(state.shape[0])
    lane = lax.broadcasted_iota(jnp.int32, (step, size), 1)
    sub = lax.broadcasted_iota(jnp.int32, (step, size), 0)
    lane_all = lax.broadcasted_iota(jnp.int32, (size, size), 1)
    for base in range(first, last, step):
        stop = base + step
        own = (lane >= base) & (lane < stop)
        for b in blocks:
            rows = state[b, base:stop, :]
            columns = [jnp.broadcast_to(rows[:, base + k : base + k + 1], (step, size)) for k in range(step)]
            unit = jnp.where(lane == sub + base, 1.0, 0.0)
            pivots = jnp.ones((step, size), jnp.float32)
            for k in range(step):
                pivot = jnp.broadcast_to(columns[k][k : k + 1, :], (step, size))
                pivots = jnp.where(sub == k, pivot, pivots)
                factor = jnp.where(sub > k, columns[k] / pivot, 0.0)
                for later in range(k + 1, step):
                    columns[later] = columns[later] - factor * jnp.broadcast_to(columns[later][k : k + 1, :], (step, size))
                rows = rows - factor * jnp.broadcast_to(rows[k : k + 1, :], (step, size))
                unit = unit - factor * jnp.broadcast_to(unit[k : k + 1, :], (step, size))
            done = jnp.where(own, unit, rows)
            if stop < size:
                lh, lm, ll = split3(rows / pivots)
                rh, rm, rl = split3(done)
                left = jnp.concatenate([lh, lh, lm, lh, ll, lm], axis=0).astype(jnp.bfloat16)
                right = jnp.concatenate([rh, rm, rh, rl, rh, rm], axis=0).astype(jnp.bfloat16)
                update = lax.dot_general(left, right, (((0,), (0,)), ((), ())), preferred_element_type=jnp.float32)
                below = state[b, stop:, :]
                inside = (lane_all[stop:] >= base) & (lane_all[stop:] < stop)
                state[b, stop:, :] = jnp.where(inside, 0.0, below) - update[stop:]
            state[b, base:stop, :] = jnp.where(lane <= sub + base, done * lax.rsqrt(pivots), 0.0)


def exact_parts(weights):
    high, mid, low = split3(weights)
    return jnp.concatenate([high, mid], axis=0).astype(jnp.bfloat16), low.astype(jnp.bfloat16)


def exact_dot(rows, parts):
    out = jnp.dot(jnp.concatenate([rows, rows], axis=1), parts[0], preferred_element_type=jnp.float32)
    return out + jnp.dot(rows, parts[1], preferred_element_type=jnp.float32)


def unpack(rows, odd):
    wide = rows.astype(jnp.float32)
    return jnp.concatenate([jnp.where(odd, 0.0, wide), jnp.where(odd, wide, 0.0)], axis=1).astype(jnp.bfloat16)


def mask_halves(out, odd):
    half = out.shape[1] // 2
    return jnp.concatenate([jnp.where(odd, 0.0, out[:, :half]), jnp.where(odd, out[:, half:], 0.0)], axis=1).astype(jnp.bfloat16)


def whole_kernel(
    count, sections, phys, bond, scale, mix_scale,
    even_ref, other_ref, stored_hbm, charge_ref,
    out_hbm, grad_ref,
    stored, ordered, packed_next, compressed_next, turned, adjoints, out, charge_own, charge_next,
    state, inverse_next, gram_part, gram_land, gram_all, cross_part, cross_land, cross_all,
    send_a, recv_a, send_b, recv_b, send_c, recv_c, send_d, recv_d, send_r, recv_r, load_sem, store_sem,
):
    me = lax.axis_index("cols")
    row = lax.axis_index("rows")
    half = bond // 2
    below = lax.rem(row + sections - 1, sections)
    above = lax.rem(row + 1, sections)

    def after(k):
        return lax.rem(me + k, count)

    def before(k):
        return lax.rem(me + count - k, count)

    barrier = pltpu.get_barrier_semaphore()
    pl.semaphore_signal(barrier, inc=1, device_id={"rows": below}, device_id_type=MESH)
    pl.semaphore_signal(barrier, inc=1, device_id={"rows": above}, device_id_type=MESH)

    @pl.loop(1, count, unroll=True)
    def _(k):
        pl.semaphore_signal(barrier, inc=1, device_id={"cols": after(k)}, device_id_type=MESH)

    load = pltpu.make_async_copy(stored_hbm, stored, load_sem)
    load.start()
    charge = charge_ref[0, 0]
    charge_own[...] = jnp.full(charge_own.shape, charge, jnp.int32)
    tile = 2 * bond
    tiles = phys // 2
    place = lax.broadcasted_iota(jnp.int32, (tile, half), 0)

    phalf = phys // 2
    lefts = tile // phalf

    def odd_rows(which, step, charge):
        left_odd = (step * lefts + place // phalf) >= charge
        return left_odd != (which == 1)

    packed = (even_ref, other_ref)
    per_half = tiles // 2

    def rows_of(step):
        return pl.ds(pl.multiple_of(step * tile, tile), tile)

    def to_below(source, target, index):
        return pltpu.make_async_remote_copy(
            src_ref=source, dst_ref=target, send_sem=send_r.at[index], recv_sem=recv_r.at[index],
            device_id={"rows": below}, device_id_type=MESH,
        )

    pieces = 4
    piece = phys * bond // pieces
    charge_down = to_below(charge_own, charge_next, pieces)
    rows_down = []
    for index in range(pieces):
        start = index * piece % (pieces // 2 * piece)
        source = packed[index * 2 // pieces].at[start : start + piece, :]
        rows_down.append(to_below(source, packed_next.at[index * piece : (index + 1) * piece, :], index))
    pl.semaphore_wait(barrier, count + 1)
    charge_down.start()
    for copy in rows_down:
        copy.start()
    lane_place = lax.broadcasted_iota(jnp.int32, (half, tile), 1)
    gram = jnp.zeros((half, bond), jnp.float32)
    for which in range(2):

        def gram_step(step, total, which=which):
            rows = packed[which][rows_of(step), :]
            across = rows.T
            flat = unpack(rows, odd_rows(which, step, charge))
            wide = across.astype(jnp.float32)
            odd = ((step * lefts + lane_place // phalf) >= charge) != (which == 1)
            columns = rows_of(which * per_half + step)
            turned[:half, columns] = jnp.where(odd, 0.0, wide).astype(jnp.bfloat16)
            turned[half:, columns] = jnp.where(odd, wide, 0.0).astype(jnp.bfloat16)
            return total + jnp.dot(across, flat, preferred_element_type=jnp.float32)

        gram = lax.fori_loop(0, per_half, gram_step, gram)
    gram_part[: count // 2] = gram[:, :half].reshape(count // 2, -1, half)
    gram_part[count // 2 :] = gram[:, half:].reshape(count // 2, -1, half)

    def scatter(k, part, land, send, recv):
        return pltpu.make_async_remote_copy(
            src_ref=part.at[after(k)], dst_ref=land.at[k], send_sem=send.at[k], recv_sem=recv.at[k],
            device_id={"cols": after(k)}, device_id_type=MESH,
        )

    def gather(k, owner, whole, send, recv):
        return pltpu.make_async_remote_copy(
            src_ref=whole.at[owner], dst_ref=whole.at[owner], send_sem=send.at[k], recv_sem=recv.at[k],
            device_id={"cols": after(k)}, device_id_type=MESH,
        )

    @pl.loop(1, count)
    def _(k):
        scatter(k, gram_part, gram_land, send_a, recv_a).start()

    gram_land[0] = gram_part[me]
    load.wait()
    group = bond // phys
    block = group * phys

    def reorder(step, source, target):
        left = pl.ds(pl.multiple_of(step * group, group), group)
        rows = source[:, left, :].astype(jnp.float32)
        rows = jnp.swapaxes(rows, 0, 1).reshape(block, rows.shape[2])
        target[pl.ds(pl.multiple_of(step * bond, bond), bond), :] = rows.T.astype(jnp.bfloat16)

    @pl.loop(0, bond // group // 2)
    def _(step):
        reorder(step, stored, ordered)

    @pl.loop(1, count)
    def _(k):
        scatter(k, gram_part, gram_land, send_a, recv_a).wait_recv()

    gram_all[me] = jnp.sum(gram_land[...], axis=0)

    @pl.loop(1, count)
    def _(k):
        gather(k, me, gram_all, send_b, recv_b).start()

    @pl.loop(bond // group // 2, bond // group)
    def _(step):
        reorder(step, stored, ordered)

    @pl.loop(1, count)
    def _(k):
        gather(k, before(k), gram_all, send_b, recv_b).wait_recv()

    state[0] = gram_all[: count // 2].reshape(half, half) * scale
    state[1] = gram_all[count // 2 :].reshape(half, half) * scale
    invert_factor(state, half, 0, half)
    inverse_down = to_below(state, inverse_next, pieces + 1)
    inverse_down.start()
    charge_down.wait_recv()
    charge_above = charge_next[0:1, :]
    cross = jnp.zeros((bond, bond), jnp.float32)
    for index in range(pieces):
        rows_down[index].wait_recv()
        first = index * piece // tile
        other = jnp.concatenate(
            [
                unpack(packed_next[step * tile : (step + 1) * tile, :], odd_rows(step // per_half, step % per_half, charge_above))
                for step in range(first, first + piece // tile)
            ],
            axis=0,
        )
        cross += jnp.dot(turned[:, index * piece : (index + 1) * piece], other, preferred_element_type=jnp.float32)
    cross_part[: count // 2] = cross[:, :half].reshape(count // 2, -1, half)
    cross_part[count // 2 :] = cross[:, half:].reshape(count // 2, -1, half)

    @pl.loop(1, count, unroll=True)
    def _(k):
        scatter(k, cross_part, cross_land, send_c, recv_c).start()

    cross_land[0] = cross_part[me]
    own = exact_parts(jnp.concatenate([state[0].T, state[1].T], axis=1))
    for which in range(2):

        @pl.loop(0, per_half)
        def _(step, which=which):
            wide = exact_dot(packed[which][rows_of(step), :], own)
            wide = mask_halves(wide, odd_rows(which, step, charge)).astype(jnp.float32)
            wide = jnp.swapaxes(wide.reshape(lefts, phalf, bond), 0, 1)
            left = pl.ds(pl.multiple_of(step * lefts, lefts), lefts)
            out[which * phalf : (which + 1) * phalf, left, :] = wide.astype(jnp.bfloat16)

    store = pltpu.make_async_copy(out, out_hbm, store_sem)
    store.start()

    @pl.loop(1, count, unroll=True)
    def _(k):
        scatter(k, cross_part, cross_land, send_c, recv_c).wait_recv()

    cross_all[me] = jnp.sum(cross_land[...], axis=0)

    @pl.loop(1, count, unroll=True)
    def _(k):
        gather(k, me, cross_all, send_d, recv_d).start()

    inverse_down.wait_recv()
    following = exact_parts(jnp.concatenate([inverse_next[0].T, inverse_next[1].T], axis=1))
    for which in range(2):

        @pl.loop(0, per_half)
        def _(step, which=which):
            rows = rows_of(which * per_half + step)
            wide = exact_dot(packed_next[rows, :], following)
            compressed_next[rows, :] = mask_halves(wide, odd_rows(which, step, charge_above))

    @pl.loop(1, count)
    def _(k):
        scatter(k, gram_part, gram_land, send_a, recv_a).wait_send()
        gather(k, me, gram_all, send_b, recv_b).wait_send()
        scatter(k, cross_part, cross_land, send_c, recv_c).wait_send()

    @pl.loop(1, count, unroll=True)
    def _(k):
        gather(k, before(k), cross_all, send_d, recv_d).wait_recv()

    total = jnp.concatenate(
        [cross_all[: count // 2].reshape(bond, half), cross_all[count // 2 :].reshape(bond, half)], axis=1
    )
    upper = jnp.concatenate(
        [
            jnp.dot(state[0], total[:half], precision=HIGH, preferred_element_type=jnp.float32),
            jnp.dot(state[1], total[half:], precision=HIGH, preferred_element_type=jnp.float32),
        ],
        axis=0,
    )
    turn = (((1,), (1,)), ((), ()))
    correlation = jnp.concatenate(
        [
            lax.dot_general(upper[:, :half], inverse_next[0], turn, precision=HIGH, preferred_element_type=jnp.float32),
            lax.dot_general(upper[:, half:], inverse_next[1], turn, precision=HIGH, preferred_element_type=jnp.float32),
        ],
        axis=1,
    )
    mixing = (correlation * mix_scale).T.astype(jnp.bfloat16)

    for step in range(pieces):
        mixed = jnp.dot(compressed_next[step * piece : (step + 1) * piece, :], mixing, preferred_element_type=jnp.float32)
        mixed = mixed.astype(jnp.bfloat16)
        which, place_in_half = divmod(step, pieces // 2)
        height = block // 2
        for part in range(piece // height):
            column = (place_in_half * (piece // height) + part) * bond
            chunk = mixed[part * height : (part + 1) * height]
            adjoints[which * height : (which + 1) * height, column : column + bond] = chunk
    pairs = jnp.dot(adjoints[...], ordered[...], preferred_element_type=jnp.float32)
    down = lax.broadcasted_iota(jnp.int32, (block, block), 0)
    across = lax.broadcasted_iota(jnp.int32, (block, block), 1)
    same = lax.rem(down, block // 2) // phalf == across // phys
    pairs = jnp.where(same, pairs, 0.0).reshape(2, group, phalf, block).sum(axis=1).reshape(phys, block)
    tall = lax.broadcasted_iota(jnp.int32, (block, phys), 0)
    wide = lax.broadcasted_iota(jnp.int32, (block, phys), 1)
    fold = jnp.where(lax.rem(tall, phys) == wide, 1.0, 0.0)
    gradient = jnp.dot(pairs, fold, precision=HIGH, preferred_element_type=jnp.float32)
    grad_ref[...] = jnp.where(row == sections - 1, 0.0, gradient / bond)
    for copy in rows_down:
        copy.wait_send()
    charge_down.wait_send()
    inverse_down.wait_send()
    store.wait()

    @pl.loop(1, count, unroll=True)
    def _(k):
        gather(k, me, cross_all, send_d, recv_d).wait_send()


def shards(boundary_in, row_operator, charges):
    stored, oper, charge = boundary_in[0, 0], row_operator[0, 0], charges[0, 0]
    phys, bond = stored.shape[0], stored.shape[2]
    half, phalf = bond // 2, phys // 2
    count, sections = lax.axis_size("cols"), lax.axis_size("rows")
    left_odd = (jnp.arange(bond) >= charge)[None, :, None]
    low, high = stored[:, :, :half], stored[:, :, half:]
    even = jnp.einsum("pq,qlc->lpc", oper[:phalf], jnp.where(left_odd, high, low), preferred_element_type=jnp.float32)
    other = jnp.einsum("pq,qlc->lpc", oper[phalf:], jnp.where(left_odd, low, high), preferred_element_type=jnp.float32)
    even = even.astype(jnp.bfloat16).reshape(-1, half)
    other = other.astype(jnp.bfloat16).reshape(-1, half)
    scale = 2.0 / (count * phys * bond)
    mix_scale = 2.0 / (bond * math.sqrt(count * phys))
    vmem = pl.BlockSpec(memory_space=pltpu.VMEM)
    gram_shape = (count, half * bond // count // half, half)
    cross_shape = (count, bond * bond // count // half, half)
    sems = pltpu.SemaphoreType.DMA((count,))
    compressed, gradient = pl.pallas_call(
        functools.partial(whole_kernel, count, sections, phys, bond, scale, mix_scale),
        out_shape=(
            jax.ShapeDtypeStruct((phys, bond, bond), jnp.bfloat16),
            jax.ShapeDtypeStruct((phys, phys), jnp.float32),
        ),
        in_specs=[vmem, vmem, pl.BlockSpec(memory_space=pl.ANY), pl.BlockSpec(memory_space=pltpu.SMEM)],
        out_specs=(pl.BlockSpec(memory_space=pl.ANY), vmem),
        scratch_shapes=[
            pltpu.VMEM((phys, bond, bond), jnp.bfloat16),
            pltpu.VMEM((phys * bond, bond), jnp.bfloat16),
            pltpu.VMEM((phys * bond, half), jnp.bfloat16),
            pltpu.VMEM((phys * bond, bond), jnp.bfloat16),
            pltpu.VMEM((bond, phys * bond), jnp.bfloat16),
            pltpu.VMEM((bond, phys * bond), jnp.bfloat16),
            pltpu.VMEM((phys, bond, bond), jnp.bfloat16),
            pltpu.VMEM((8, half), jnp.int32),
            pltpu.VMEM((8, half), jnp.int32),
            pltpu.VMEM((2, half, half), jnp.float32),
            pltpu.VMEM((2, half, half), jnp.float32),
            pltpu.VMEM(gram_shape, jnp.float32),
            pltpu.VMEM(gram_shape, jnp.float32),
            pltpu.VMEM(gram_shape, jnp.float32),
            pltpu.VMEM(cross_shape, jnp.float32),
            pltpu.VMEM(cross_shape, jnp.float32),
            pltpu.VMEM(cross_shape, jnp.float32),
            sems, sems, sems, sems, sems, sems, sems, sems,
            pltpu.SemaphoreType.DMA((6,)),
            pltpu.SemaphoreType.DMA((6,)),
            pltpu.SemaphoreType.DMA,
            pltpu.SemaphoreType.DMA,
        ],
        compiler_params=pltpu.CompilerParams(collective_id=0, has_side_effects=True),
        name="orthonormalise",
    )(even, other, stored, charges)
    return (compressed.reshape(boundary_in.shape), gradient[None, None])


def solution(mesh):
    return jax.shard_map(
        shards,
        mesh=mesh,
        in_specs=(
            P("rows", "cols", None, None, None),
            P("rows", "cols", None, None),
            P("rows", "cols"),
        ),
        out_specs=(P("rows", "cols", None, None, None), P("rows", "cols", None, None)),
        check_vma=False,
    )
```
